32 devices in a mesh: row: 4 (over x, core), col: 2 (over y), reg: 4 (over z).
Axes of the slice: x: 2, y: 2, z: 4, core: 2. Of those that a mesh axis runs over, the one named last changes fastest.
Arguments:
- activity: bfloat16 [24576, 2048], P(('row', 'col', 'reg')), may hold values from -6 to 6
- basis: bfloat16 [24576, 64], P(('row', 'col', 'reg')), may hold values from -0.21875 to 0.21875
- region_of: int32 [192], P(('row', 'col', 'reg')), may hold values from 0 to 3
- pairs: int32 [1024, 2], P(('row', 'col', 'reg')), may hold values from 0 to 15, as said below
- lags: int32 [8], replicated, may hold values from 0 to 7, each once
Outputs:
- covariance: bfloat16 [1024, 64, 512], P(('row', 'col', 'reg'))
The draws below stay inside these ranges and needn't reach their ends.
Inputs may be any that keep to these rules, and one draw needn't show every extreme that they name: pairs[p, 0] is below 8 and pairs[p, 1] below 16.
All inputs are finite; a program needn't handle non-finite values.
Results may differ from the reference program's by a relative error of at most 0.0055.
Values may be sent and summed in bfloat16 or wider, within the bound.
A program may use at most 128 MiB of HBM per device.

```python
import jax
import jax.numpy as jnp
from jax import lax

K = 64
BLK = 128
NLAG = 8
NDEV = 768
TB = 2048
PAIR_DEV = 32
NEURONS = 24576
NBLK = 192
NPAIRS = 1024
CELLREG = 4
LEFTS = 8
RIGHTS = 16
N_ROW = 4
N_COL = 2
N_REG = 4


def draw_pairs(key, part):
    first = jax.random.fold_in(key, 11)
    second = jax.random.fold_in(key, 23)
    left = jax.random.randint(first, (NPAIRS, 1), 0, LEFTS, dtype=jnp.int32)
    right = jax.random.randint(second, (NPAIRS, 1), 0, RIGHTS, dtype=jnp.int32)
    return jnp.concatenate([left, right], axis=1)


def plant(result, stream_key, least, top_value):
    index_at = [jax.random.randint(jax.random.fold_in(stream_key, axis), (), 0, length) for axis, length in enumerate(result.shape)]
    widest = result.shape.index(max(result.shape))
    beside = index_at[:widest] + [(index_at[widest] + 1) % result.shape[widest]] + index_at[widest + 1:]
    return result.at[tuple(index_at)].set(least).at[tuple(beside)].set(top_value)


def shard_levels(key, extent, cuts, low, high):
    def one(axis_at, parts):
        draws = jax.random.uniform(jax.random.fold_in(jax.random.fold_in(key, 6), axis_at), (parts,), jnp.float32, low / len(cuts), high / len(cuts))
        return jnp.repeat(jnp.exp(draws), extent[axis_at] // parts).reshape((-1,) + (1,) * (len(extent) - axis_at - 1))

    level = one(*cuts[0])
    for cut in cuts[1:]:
        level = level * one(*cut)
    return level


def gaussian(own_key, extent, scale, limit, split=(), held_as=jnp.bfloat16):
    factor_of = shard_levels(own_key, extent, split, -0.22, 0.18) if split else 1.0
    drawn = jax.random.normal(own_key, extent, jnp.float32) * scale * factor_of
    return jnp.minimum(jnp.maximum(drawn, -limit), limit).astype(held_as)


def setup_inputs(seed: int = 0) -> dict:
    streams_of = jax.random.split(jax.random.key(seed), 6)
    activity = gaussian(streams_of[0], (NEURONS, TB), 1.0, 6.0, ((0, 32),))
    basis = gaussian(streams_of[1], (NEURONS, K), NDEV ** -0.5, 0.21875, ((0, 32),))
    region_of = plant(jax.random.randint(streams_of[2], (NBLK,), 0, CELLREG), jax.random.fold_in(streams_of[2], 1), 0, CELLREG - 1).astype(jnp.int32)
    pairs = draw_pairs(jax.random.fold_in(streams_of[5], 71), 0)
    lags = jax.random.permutation(streams_of[4], NLAG).astype(jnp.int32)
    return {"activity": activity, "basis": basis, "region_of": region_of, "pairs": pairs, "lags": lags}


def reference(activity, basis, region_of, pairs, lags):
    cells = N_ROW * N_COL
    per_cell = N_REG * NDEV // BLK
    act = activity.reshape(cells, per_cell * BLK, TB)
    bas = basis.reshape(cells, per_cell * BLK, K)
    rid = jnp.repeat(region_of.reshape(cells, per_cell), BLK, axis=1)

    def cell_signal(args):
        a, b, r = args
        match = r[:, None] == lax.iota(jnp.int32, N_REG)[None, :]
        masked = jnp.where(match[:, :, None], b[:, None, :], jnp.zeros((), jnp.bfloat16))
        masked = masked.reshape(per_cell * BLK, N_REG * K)
        return lax.dot_general(masked, a, (((0,), (0,)), ((), ())), preferred_element_type=jnp.float32)

    panel = lax.map(cell_signal, (act, bas, rid)).reshape(cells * N_REG, K, TB).astype(jnp.bfloat16)
    index = lax.iota(jnp.int32, NPAIRS)
    device = index // PAIR_DEV
    row_id = device // (N_COL * N_REG)
    col_id = (device // N_REG) % N_COL
    left = row_id * (N_COL * N_REG) + pairs[:, 0]
    right = ((pairs[:, 1] // N_REG) * N_COL + col_id) * N_REG + pairs[:, 1] % N_REG
    padded = jnp.pad(panel, ((0, 0), (0, 0), (0, NLAG)))
    scale = 1.0 / (TB ** 0.5)

    def one_pair(args):
        l, r = args
        left_panel = panel[l]
        right_panel = padded[r]
        stack = jnp.stack([lax.dynamic_slice_in_dim(right_panel, lags[m], TB, 1) for m in range(NLAG)])
        stack = stack.reshape(NLAG * K, TB)
        prod = lax.dot_general(left_panel, stack, (((1,), (1,)), ((), ())), preferred_element_type=jnp.float32)
        return (prod * scale).astype(jnp.bfloat16)

    return lax.map(one_pair, (left, right))
```

```python
import functools

import jax
import jax.numpy as jnp
from jax import lax
from jax.experimental import pallas as pl
from jax.experimental.pallas import tpu as pltpu
from jax.sharding import PartitionSpec as P

BLK = 128


def shift_right(x, s):
    col = lax.broadcasted_iota(jnp.int32, x.shape, 1)
    return jnp.where(col >= s, pltpu.roll(x, s, 1), 0.0)


def shift_left(x, s):
    bins = x.shape[1]
    col = lax.broadcasted_iota(jnp.int32, x.shape, 1)
    return jnp.where(col < bins - s, pltpu.roll(x, bins - s, 1), 0.0)


def pair_kernel(nlag, pairs_ref, lags_ref, left_ref, right_ref, out_ref, prod):
    left, right = left_ref[0], right_ref[0]
    width, bins = left.shape
    leftf, rightf = left.astype(jnp.float32), right.astype(jnp.float32)
    lhs = jnp.concatenate([left, shift_right(leftf, 1).astype(jnp.bfloat16)], axis=0)
    rhs = jnp.concatenate(
        [right] + [shift_left(rightf, s).astype(jnp.bfloat16) for s in range(2, nlag, 2)], axis=0
    )
    acc = lax.dot_general(
        lhs, rhs, (((1,), (1,)), ((), ())), preferred_element_type=jnp.float32
    )
    acc = acc * (1.0 / bins**0.5)
    for lag in range(nlag):
        m1, m2 = lag % 2, lag // 2
        prod[lag] = acc[m1 * width:(m1 + 1) * width, m2 * width:(m2 + 1) * width]
    out_ref[0] = jnp.concatenate(
        [prod[lags_ref[m]] for m in range(nlag)], axis=1
    ).astype(jnp.bfloat16)


def covariances(lefts, rights, pairs, lags):
    npairs = pairs.shape[0]
    nlag = lags.shape[0]
    _, width, bins = lefts.shape
    return pl.pallas_call(
        functools.partial(pair_kernel, nlag),
        grid_spec=pltpu.PrefetchScalarGridSpec(
            num_scalar_prefetch=2,
            grid=(npairs,),
            in_specs=[
                pl.BlockSpec((1, width, bins), lambda p, pairs, lags: (pairs[p, 0], 0, 0)),
                pl.BlockSpec((1, width, bins), lambda p, pairs, lags: (pairs[p, 1], 0, 0)),
            ],
            out_specs=pl.BlockSpec((1, width, nlag * width), lambda p, pairs, lags: (p, 0, 0)),
            scratch_shapes=[pltpu.VMEM((nlag, width, width), jnp.float32)],
        ),
        out_shape=jax.ShapeDtypeStruct((npairs, width, nlag * width), jnp.bfloat16),
        compiler_params=pltpu.CompilerParams(dimension_semantics=("arbitrary",)),
    )(pairs, lags, lefts, rights)


def local(nreg, activity, basis, region_of, pairs, lags):
    width = basis.shape[1]
    bins = activity.shape[1]
    row_region = jnp.repeat(region_of, BLK)
    match = row_region[:, None] == jnp.arange(nreg, dtype=jnp.int32)[None, :]
    masked = jnp.where(match[:, :, None], basis[:, None, :], jnp.zeros((), jnp.bfloat16))
    masked = masked.reshape(basis.shape[0], nreg * width)
    partial = lax.dot_general(
        masked, activity, (((0,), (0,)), ((), ())), preferred_element_type=jnp.float32
    )
    signal = lax.psum_scatter(partial, "reg", scatter_dimension=0, tiled=True)
    panel = signal.reshape(1, width, bins).astype(jnp.bfloat16)
    lefts = lax.all_gather(panel, ("col", "reg"), axis=0, tiled=True)
    rights = lax.all_gather(panel, ("row", "reg"), axis=0, tiled=True)
    return covariances(lefts, rights, pairs, lags)


def solution(mesh):
    return jax.shard_map(
        functools.partial(local, mesh.shape["reg"]),
        mesh=mesh,
        in_specs=(
            P(("row", "col", "reg"), None),
            P(("row", "col", "reg"), None),
            P(("row", "col", "reg")),
            P(("row", "col", "reg"), None),
            P(),
        ),
        out_specs=P(("row", "col", "reg"), None, None),
        check_vma=False,
    )
```

```python
import functools

import jax
import jax.numpy as jnp
from jax import lax
from jax.experimental import pallas as pl
from jax.experimental.pallas import tpu as pltpu
from jax.sharding import PartitionSpec as P

BLK = 128
CHUNKS = 2


def shift_right(x, s):
    col = lax.broadcasted_iota(jnp.int32, x.shape, 1)
    return jnp.where(col >= s, pltpu.roll(x, s, 1), 0.0)


def shift_left(x, s):
    bins = x.shape[1]
    col = lax.broadcasted_iota(jnp.int32, x.shape, 1)
    return jnp.where(col < bins - s, pltpu.roll(x, bins - s, 1), 0.0)


def pair_kernel(nlag, pairs_ref, lags_ref, left_ref, right_ref, out_ref, prod):
    left, right = left_ref[0], right_ref[0]
    width, bins = left.shape
    leftf, rightf = left.astype(jnp.float32), right.astype(jnp.float32)
    lhs = jnp.concatenate([left, shift_right(leftf, 1).astype(jnp.bfloat16)], axis=0)
    rhs = jnp.concatenate(
        [right] + [shift_left(rightf, s).astype(jnp.bfloat16) for s in range(2, nlag, 2)], axis=0
    )
    acc = lax.dot_general(
        lhs, rhs, (((1,), (1,)), ((), ())), preferred_element_type=jnp.float32
    )
    acc = acc * (1.0 / bins**0.5)
    for lag in range(nlag):
        m1, m2 = lag % 2, lag // 2
        prod[lag] = acc[m1 * width:(m1 + 1) * width, m2 * width:(m2 + 1) * width]
    out_ref[0] = jnp.concatenate(
        [prod[lags_ref[m]] for m in range(nlag)], axis=1
    ).astype(jnp.bfloat16)


def covariances(lefts, rights, pairs, lags):
    npairs = pairs.shape[0]
    nlag = lags.shape[0]
    _, width, bins = lefts.shape
    return pl.pallas_call(
        functools.partial(pair_kernel, nlag),
        grid_spec=pltpu.PrefetchScalarGridSpec(
            num_scalar_prefetch=2,
            grid=(npairs,),
            in_specs=[
                pl.BlockSpec((1, width, bins), lambda p, pairs, lags: (pairs[p, 0], 0, 0)),
                pl.BlockSpec((1, width, bins), lambda p, pairs, lags: (pairs[p, 1], 0, 0)),
            ],
            out_specs=pl.BlockSpec((1, width, nlag * width), lambda p, pairs, lags: (p, 0, 0)),
            scratch_shapes=[pltpu.VMEM((nlag, width, width), jnp.float32)],
        ),
        out_shape=jax.ShapeDtypeStruct((npairs, width, nlag * width), jnp.bfloat16),
        compiler_params=pltpu.CompilerParams(dimension_semantics=("arbitrary",)),
    )(pairs, lags, lefts, rights)


def panels_kernel(
    shape, chunks, region_ref, basis_ref, act_ref, lefts_ref, rights_ref,
    own, send, landed, stage,
    rs_send, rs_recv, reg_send, reg_recv, col_send, col_recv,
    x_send, x_recv, sib_send, sib_recv, fwd_send, fwd_recv, left_sem, right_sem,
):
    nrow, ncol, nreg = shape
    nx = nrow // 2
    width = basis_ref.shape[1]
    bins = act_ref.shape[1]
    span = bins // chunks
    i, j, g = lax.axis_index("row"), lax.axis_index("col"), lax.axis_index("reg")
    x, core = i // 2, i % 2
    sib = x * 2 + 1 - core

    def reg_at(k):
        return {"reg": (g + k) % nreg}

    def col_at(k):
        return {"col": (j + k) % ncol}

    def x_at(k):
        return {"row": ((x + k) % nx) * 2 + core}

    peers = [reg_at(k) for k in range(1, nreg)]
    peers += [col_at(k) for k in range(1, ncol)]
    peers += [x_at(k) for k in range(1, nx)]
    peers += [{"row": sib}]
    barrier = pltpu.get_barrier_semaphore()
    for peer in peers:
        pl.semaphore_signal(
            barrier, inc=1, device_id=peer, device_id_type=pl.DeviceIdType.MESH
        )

    def remote(src, dst, send_sem, recv_sem, peer):
        return pltpu.make_async_remote_copy(
            src_ref=src, dst_ref=dst, send_sem=send_sem, recv_sem=recv_sem,
            device_id=peer, device_id_type=pl.DeviceIdType.MESH,
        )

    sent = []

    def start(*args):
        copy = remote(*args)
        copy.start()
        sent.append(copy)

    def right(row, region, c):
        return rights_ref.at[row * nreg + region, :, pl.ds(c * span, span)]

    def left(col, region, c):
        return lefts_ref.at[col * nreg + region, :, pl.ds(c * span, span)]

    pieces = []
    for n in range(basis_ref.shape[0] // BLK):
        block = basis_ref[n * BLK:(n + 1) * BLK, :]
        pieces.append(jnp.concatenate(
            [jnp.where(region_ref[n] == r, block, jnp.zeros_like(block)) for r in range(nreg)],
            axis=1,
        ))
    masked = jnp.concatenate(pieces, axis=0)

    for c in range(chunks):
        part = lax.dot_general(
            masked, act_ref[:, c * span:(c + 1) * span], (((0,), (0,)), ((), ())),
            preferred_element_type=jnp.float32,
        )
        own[c] = part
        send[c] = part.astype(jnp.bfloat16)
        if c == 0:
            pl.semaphore_wait(barrier, len(peers))
        for k in range(1, nreg):
            rows = pl.ds(pl.multiple_of((g + k) % nreg * width, width), width)
            start(
                send.at[c, rows, :], landed.at[k - 1, c],
                rs_send.at[k - 1, c], rs_recv.at[k - 1, c], reg_at(k),
            )

    def spread(src, region, q, c):
        for k in range(1, nx):
            start(src, right(i, region, c), x_send.at[k - 1, q, c], x_recv.at[k - 1, q, c], x_at(k))
        for k in range(1, ncol):
            start(src, left(j, region, c), col_send.at[k - 1, q, c], col_recv.at[k - 1, q, c], col_at(k))
        start(src, right(i, region, c), sib_send.at[q, c], sib_recv.at[q, c], {"row": sib})
        copy = pltpu.make_async_copy(src, left(j, region, c), left_sem.at[q, c])
        copy.start()
        return copy

    kept = []
    for c in range(chunks):
        total = own[c, pl.ds(pl.multiple_of(g * width, width), width), :]
        for k in range(1, nreg):
            remote(
                landed.at[k - 1, c], landed.at[k - 1, c],
                rs_send.at[k - 1, c], rs_recv.at[k - 1, c], reg_at(k),
            ).wait_recv()
            total = total + landed[k - 1, c].astype(jnp.float32)
        stage[c] = total.astype(jnp.bfloat16)
        for k in range(1, nreg):
            start(
                stage.at[c], right(i, g, c),
                reg_send.at[k - 1, c], reg_recv.at[k - 1, c], reg_at(k),
            )
        copy = pltpu.make_async_copy(stage.at[c], right(i, g, c), right_sem.at[c])
        copy.start()
        kept += [copy, spread(stage.at[c], g, 0, c)]

    def region_at(q):
        return (g - q + nreg) % nreg

    for c in range(chunks):
        for q in range(1, nreg):
            here = right(i, region_at(q), c)
            remote(here, here, reg_send.at[q - 1, c], reg_recv.at[q - 1, c], reg_at(q)).wait_recv()
            kept.append(spread(here, region_at(q), q, c))

    for c in range(chunks):
        for q in range(nreg):
            for k in range(1, nx):
                here = right((x - k + nx) % nx * 2 + core, region_at(q), c)
                remote(here, here, x_send.at[k - 1, q, c], x_recv.at[k - 1, q, c], x_at(k)).wait_recv()
                start(
                    here, here, fwd_send.at[k - 1, q, c], fwd_recv.at[k - 1, q, c], {"row": sib}
                )

    for c in range(chunks):
        for q in range(nreg):
            region = region_at(q)
            for k in range(1, ncol):
                here = left((j - k + ncol) % ncol, region, c)
                remote(here, here, col_send.at[k - 1, q, c], col_recv.at[k - 1, q, c], col_at(k)).wait_recv()
            here = right(sib, region, c)
            remote(here, here, sib_send.at[q, c], sib_recv.at[q, c], {"row": sib}).wait_recv()
            for k in range(1, nx):
                here = right((x - k + nx) % nx * 2 + 1 - core, region, c)
                remote(here, here, fwd_send.at[k - 1, q, c], fwd_recv.at[k - 1, q, c], {"row": sib}).wait_recv()
    for copy in sent:
        copy.wait_send()
    for copy in kept:
        copy.wait()


def gathered_panels(shape, activity, basis, region_of):
    nrow, ncol, nreg = shape
    nx = nrow // 2
    width, bins = basis.shape[1], activity.shape[1]
    chunks = CHUNKS
    span = bins // chunks
    dma = pltpu.SemaphoreType.DMA
    return pl.pallas_call(
        functools.partial(panels_kernel, shape, chunks),
        in_specs=[
            pl.BlockSpec(memory_space=pltpu.SMEM),
            pl.BlockSpec(memory_space=pltpu.VMEM),
            pl.BlockSpec(memory_space=pltpu.VMEM),
        ],
        out_specs=[pl.BlockSpec(memory_space=pl.ANY)] * 2,
        out_shape=[
            jax.ShapeDtypeStruct((ncol * nreg, width, bins), jnp.bfloat16),
            jax.ShapeDtypeStruct((nrow * nreg, width, bins), jnp.bfloat16),
        ],
        scratch_shapes=[
            pltpu.VMEM((chunks, nreg * width, span), jnp.float32),
            pltpu.VMEM((chunks, nreg * width, span), jnp.bfloat16),
            pltpu.VMEM((nreg - 1, chunks, width, span), jnp.bfloat16),
            pltpu.VMEM((chunks, width, span), jnp.bfloat16),
        ]
        + [dma((nreg - 1, chunks))] * 4
        + [dma((ncol - 1, nreg, chunks))] * 2
        + [dma((nx - 1, nreg, chunks))] * 2
        + [dma((nreg, chunks))] * 2
        + [dma((nx - 1, nreg, chunks))] * 2
        + [dma((nreg, chunks)), dma((chunks,))],
        compiler_params=pltpu.CompilerParams(
            collective_id=0, has_side_effects=True, vmem_limit_bytes=40 << 20
        ),
    )(region_of, basis, activity)


def local(shape, activity, basis, region_of, pairs, lags):
    lefts, rights = gathered_panels(shape, activity, basis, region_of)
    return covariances(lefts, rights, pairs, lags)


def solution(mesh):
    shape = (mesh.shape["row"], mesh.shape["col"], mesh.shape["reg"])
    return jax.shard_map(
        functools.partial(local, shape),
        mesh=mesh,
        in_specs=(
            P(("row", "col", "reg"), None),
            P(("row", "col", "reg"), None),
            P(("row", "col", "reg")),
            P(("row", "col", "reg"), None),
            P(),
        ),
        out_specs=P(("row", "col", "reg"), None, None),
        check_vma=False,
    )
```

```python
import functools

import jax
import jax.numpy as jnp
from jax import lax
from jax.experimental import pallas as pl
from jax.experimental.pallas import tpu as pltpu
from jax.sharding import PartitionSpec as P

BLK = 128
CHUNKS = 2


def shifted(x, s):
    bins = x.shape[1]
    moved = pltpu.roll(x, (bins - s) % bins, 1)
    edge = moved[:, bins - BLK:] if s > 0 else moved[:, :BLK]
    col = lax.broadcasted_iota(jnp.int32, edge.shape, 1)
    if s > 0:
        edge = jnp.where(col < BLK - s, edge, jnp.zeros_like(edge))
        return jnp.concatenate([moved[:, :bins - BLK], edge], axis=1)
    edge = jnp.where(col >= -s, edge, jnp.zeros_like(edge))
    return jnp.concatenate([edge, moved[:, BLK:]], axis=1)


def left_stack(left):
    return [left, shifted(left, -1)]


def right_stack(right, nlag):
    return [right] + [shifted(right, s) for s in range(2, nlag, 2)]


def one_pair(nlag, lags_ref, lhs, rhs, prod):
    width, bins = lhs.shape[0] // 2, lhs.shape[1]
    acc = lax.dot_general(
        lhs, rhs, (((1,), (1,)), ((), ())), preferred_element_type=jnp.float32
    )
    acc = acc * (1.0 / bins**0.5)
    for lag in range(nlag):
        m1, m2 = lag % 2, lag // 2
        prod[lag] = acc[m1 * width:(m1 + 1) * width, m2 * width:(m2 + 1) * width]
    return jnp.concatenate([prod[lags_ref[m]] for m in range(nlag)], axis=1).astype(jnp.bfloat16)


def pair_kernel(nlag, group, pairs_ref, lags_ref, lefts_ref, rights_ref, out_ref, lhs, rhs, prod):
    width = lefts_ref.shape[1]
    step = pl.program_id(0)

    @pl.when(step == 0)
    def _():
        @pl.loop(0, lefts_ref.shape[0])
        def _(r):
            for m, x in enumerate(left_stack(lefts_ref[r])):
                lhs[r, m * width:(m + 1) * width, :] = x

        @pl.loop(0, rights_ref.shape[0])
        def _(r):
            for m, x in enumerate(right_stack(rights_ref[r], nlag)):
                rhs[r, m * width:(m + 1) * width, :] = x

    for q in range(group):
        p = step * group + q
        out_ref[q] = one_pair(
            nlag, lags_ref, lhs[pairs_ref[p, 0]], rhs[pairs_ref[p, 1]], prod.at[q]
        )


def stream_kernel(nlag, pairs_ref, lags_ref, left_ref, right_ref, out_ref, prod):
    lhs = jnp.concatenate(left_stack(left_ref[0]), axis=0)
    rhs = jnp.concatenate(right_stack(right_ref[0], nlag), axis=0)
    out_ref[0] = one_pair(nlag, lags_ref, lhs, rhs, prod)


def covariances(lefts, rights, pairs, lags):
    npairs = pairs.shape[0]
    nlag = lags.shape[0]
    _, width, bins = lefts.shape
    out_shape = jax.ShapeDtypeStruct((npairs, width, nlag * width), jnp.bfloat16)
    panels = 3 * lefts.shape[0] + 5 * rights.shape[0]
    params = pltpu.CompilerParams(
        dimension_semantics=("arbitrary",), vmem_limit_bytes=48 << 20
    )
    if panels * width * bins * 2 <= 36 << 20:
        group = 4
        return pl.pallas_call(
            functools.partial(pair_kernel, nlag, group),
            grid_spec=pltpu.PrefetchScalarGridSpec(
                num_scalar_prefetch=2,
                grid=(npairs // group,),
                in_specs=[pl.BlockSpec(memory_space=pltpu.VMEM)] * 2,
                out_specs=pl.BlockSpec(
                    (group, width, nlag * width), lambda p, pairs, lags: (p, 0, 0)
                ),
                scratch_shapes=[
                    pltpu.VMEM((lefts.shape[0], 2 * width, bins), jnp.bfloat16),
                    pltpu.VMEM((rights.shape[0], nlag // 2 * width, bins), jnp.bfloat16),
                    pltpu.VMEM((group, nlag, width, width), jnp.float32),
                ],
            ),
            out_shape=out_shape,
            compiler_params=params,
        )(pairs, lags, lefts, rights)
    return pl.pallas_call(
        functools.partial(stream_kernel, nlag),
        grid_spec=pltpu.PrefetchScalarGridSpec(
            num_scalar_prefetch=2,
            grid=(npairs,),
            in_specs=[
                pl.BlockSpec((1, width, bins), lambda p, pairs, lags: (pairs[p, 0], 0, 0)),
                pl.BlockSpec((1, width, bins), lambda p, pairs, lags: (pairs[p, 1], 0, 0)),
            ],
            out_specs=pl.BlockSpec((1, width, nlag * width), lambda p, pairs, lags: (p, 0, 0)),
            scratch_shapes=[pltpu.VMEM((nlag, width, width), jnp.float32)],
        ),
        out_shape=out_shape,
        compiler_params=params,
    )(pairs, lags, lefts, rights)


def panels_kernel(
    shape, chunks, region_ref, basis_ref, act_ref, lefts_ref, rights_ref,
    own, send, landed, stage,
    rs_send, rs_recv, reg_send, reg_recv, col_send, col_recv,
    x_send, x_recv, sib_send, sib_recv, fwd_send, fwd_recv, left_sem, right_sem,
):
    nrow, ncol, nreg = shape
    nx = nrow // 2
    width = basis_ref.shape[1]
    bins = act_ref.shape[1]
    span = bins // chunks
    i, j, g = lax.axis_index("row"), lax.axis_index("col"), lax.axis_index("reg")
    x, core = i // 2, i % 2
    sib = x * 2 + 1 - core

    def reg_at(k):
        return {"reg": (g + k) % nreg}

    def col_at(k):
        return {"col": (j + k) % ncol}

    def x_at(k):
        return {"row": ((x + k) % nx) * 2 + core}

    peers = [reg_at(k) for k in range(1, nreg)]
    peers += [col_at(k) for k in range(1, ncol)]
    peers += [x_at(k) for k in range(1, nx)]
    peers += [{"row": sib}]
    barrier = pltpu.get_barrier_semaphore()
    for peer in peers:
        pl.semaphore_signal(
            barrier, inc=1, device_id=peer, device_id_type=pl.DeviceIdType.MESH
        )

    def remote(src, dst, send_sem, recv_sem, peer):
        return pltpu.make_async_remote_copy(
            src_ref=src, dst_ref=dst, send_sem=send_sem, recv_sem=recv_sem,
            device_id=peer, device_id_type=pl.DeviceIdType.MESH,
        )

    sent = []

    def start(*args):
        copy = remote(*args)
        copy.start()
        sent.append(copy)

    def right(row, region, c):
        return rights_ref.at[row * nreg + region, :, pl.ds(c * span, span)]

    def left(col, region, c):
        return lefts_ref.at[col * nreg + region, :, pl.ds(c * span, span)]

    pieces = []
    for n in range(basis_ref.shape[0] // BLK):
        block = basis_ref[n * BLK:(n + 1) * BLK, :]
        pieces.append(jnp.concatenate(
            [jnp.where(region_ref[n] == r, block, jnp.zeros_like(block)) for r in range(nreg)],
            axis=1,
        ))
    masked = jnp.concatenate(pieces, axis=0)

    for c in range(chunks):
        part = lax.dot_general(
            masked, act_ref[:, c * span:(c + 1) * span], (((0,), (0,)), ((), ())),
            preferred_element_type=jnp.float32,
        )
        own[c] = part
        send[c] = part.astype(jnp.bfloat16)
        if c == 0:
            pl.semaphore_wait(barrier, len(peers))
        for k in range(1, nreg):
            rows = pl.ds(pl.multiple_of((g + k) % nreg * width, width), width)
            start(
                send.at[c, rows, :], landed.at[k - 1, c],
                rs_send.at[k - 1, c], rs_recv.at[k - 1, c], reg_at(k),
            )

    def spread(src, region, q, c):
        for k in range(1, nx):
            start(src, right(i, region, c), x_send.at[k - 1, q, c], x_recv.at[k - 1, q, c], x_at(k))
        for k in range(1, ncol):
            start(src, left(j, region, c), col_send.at[k - 1, q, c], col_recv.at[k - 1, q, c], col_at(k))
        start(src, right(i, region, c), sib_send.at[q, c], sib_recv.at[q, c], {"row": sib})
        copy = pltpu.make_async_copy(src, left(j, region, c), left_sem.at[q, c])
        copy.start()
        return copy

    kept = []
    for c in range(chunks):
        total = own[c, pl.ds(pl.multiple_of(g * width, width), width), :]
        for k in range(1, nreg):
            remote(
                landed.at[k - 1, c], landed.at[k - 1, c],
                rs_send.at[k - 1, c], rs_recv.at[k - 1, c], reg_at(k),
            ).wait_recv()
            total = total + landed[k - 1, c].astype(jnp.float32)
        stage[c] = total.astype(jnp.bfloat16)
        for k in range(1, nreg):
            start(
                stage.at[c], right(i, g, c),
                reg_send.at[k - 1, c], reg_recv.at[k - 1, c], reg_at(k),
            )
        copy = pltpu.make_async_copy(stage.at[c], right(i, g, c), right_sem.at[c])
        copy.start()
        kept += [copy, spread(stage.at[c], g, 0, c)]

    def region_at(q):
        return (g - q + nreg) % nreg

    for c in range(chunks):
        for q in range(1, nreg):
            here = right(i, region_at(q), c)
            remote(here, here, reg_send.at[q - 1, c], reg_recv.at[q - 1, c], reg_at(q)).wait_recv()
            kept.append(spread(here, region_at(q), q, c))

    for c in range(chunks):
        for q in range(nreg):
            for k in range(1, nx):
                here = right((x - k + nx) % nx * 2 + core, region_at(q), c)
                remote(here, here, x_send.at[k - 1, q, c], x_recv.at[k - 1, q, c], x_at(k)).wait_recv()
                start(
                    here, here, fwd_send.at[k - 1, q, c], fwd_recv.at[k - 1, q, c], {"row": sib}
                )

    for c in range(chunks):
        for q in range(nreg):
            region = region_at(q)
            for k in range(1, ncol):
                here = left((j - k + ncol) % ncol, region, c)
                remote(here, here, col_send.at[k - 1, q, c], col_recv.at[k - 1, q, c], col_at(k)).wait_recv()
            here = right(sib, region, c)
            remote(here, here, sib_send.at[q, c], sib_recv.at[q, c], {"row": sib}).wait_recv()
            for k in range(1, nx):
                here = right((x - k + nx) % nx * 2 + 1 - core, region, c)
                remote(here, here, fwd_send.at[k - 1, q, c], fwd_recv.at[k - 1, q, c], {"row": sib}).wait_recv()
    for copy in sent:
        copy.wait_send()
    for copy in kept:
        copy.wait()


def gathered_panels(shape, activity, basis, region_of):
    nrow, ncol, nreg = shape
    nx = nrow // 2
    width, bins = basis.shape[1], activity.shape[1]
    chunks = CHUNKS
    span = bins // chunks
    dma = pltpu.SemaphoreType.DMA
    return pl.pallas_call(
        functools.partial(panels_kernel, shape, chunks),
        in_specs=[
            pl.BlockSpec(memory_space=pltpu.SMEM),
            pl.BlockSpec(memory_space=pltpu.VMEM),
            pl.BlockSpec(memory_space=pltpu.VMEM),
        ],
        out_specs=[pl.BlockSpec(memory_space=pl.ANY)] * 2,
        out_shape=[
            jax.ShapeDtypeStruct((ncol * nreg, width, bins), jnp.bfloat16),
            jax.ShapeDtypeStruct((nrow * nreg, width, bins), jnp.bfloat16),
        ],
        scratch_shapes=[
            pltpu.VMEM((chunks, nreg * width, span), jnp.float32),
            pltpu.VMEM((chunks, nreg * width, span), jnp.bfloat16),
            pltpu.VMEM((nreg - 1, chunks, width, span), jnp.bfloat16),
            pltpu.VMEM((chunks, width, span), jnp.bfloat16),
        ]
        + [dma((nreg - 1, chunks))] * 4
        + [dma((ncol - 1, nreg, chunks))] * 2
        + [dma((nx - 1, nreg, chunks))] * 2
        + [dma((nreg, chunks))] * 2
        + [dma((nx - 1, nreg, chunks))] * 2
        + [dma((nreg, chunks)), dma((chunks,))],
        compiler_params=pltpu.CompilerParams(
            collective_id=0, has_side_effects=True, vmem_limit_bytes=40 << 20
        ),
    )(region_of, basis, activity)


def local(shape, activity, basis, region_of, pairs, lags):
    lefts, rights = gathered_panels(shape, activity, basis, region_of)
    return covariances(lefts, rights, pairs, lags)


def solution(mesh):
    shape = (mesh.shape["row"], mesh.shape["col"], mesh.shape["reg"])
    return jax.shard_map(
        functools.partial(local, shape),
        mesh=mesh,
        in_specs=(
            P(("row", "col", "reg"), None),
            P(("row", "col", "reg"), None),
            P(("row", "col", "reg")),
            P(("row", "col", "reg"), None),
            P(),
        ),
        out_specs=P(("row", "col", "reg"), None, None),
        check_vma=False,
    )
```

```python
import functools

import jax
import jax.numpy as jnp
from jax import lax
from jax.experimental import pallas as pl
from jax.experimental.pallas import tpu as pltpu
from jax.sharding import PartitionSpec as P

BLK = 128
CHUNKS = 4


def shifted(x, s):
    bins = x.shape[1]
    moved = pltpu.roll(x, (bins - s) % bins, 1)
    edge = moved[:, bins - BLK:] if s > 0 else moved[:, :BLK]
    col = lax.broadcasted_iota(jnp.int32, edge.shape, 1)
    if s > 0:
        edge = jnp.where(col < BLK - s, edge, jnp.zeros_like(edge))
        return jnp.concatenate([moved[:, :bins - BLK], edge], axis=1)
    edge = jnp.where(col >= -s, edge, jnp.zeros_like(edge))
    return jnp.concatenate([edge, moved[:, BLK:]], axis=1)


def left_stack(left):
    return [left, shifted(left, -1)]


def right_stack(right, nlag):
    return [right] + [shifted(right, s) for s in range(2, nlag, 2)]


def one_pair(nlag, lags_ref, lhs, rhs, prod):
    width, bins = lhs.shape[0] // 2, lhs.shape[1]
    acc = lax.dot_general(
        lhs, rhs, (((1,), (1,)), ((), ())), preferred_element_type=jnp.float32
    )
    acc = acc * (1.0 / bins**0.5)
    for lag in range(nlag):
        m1, m2 = lag % 2, lag // 2
        prod[lag] = acc[m1 * width:(m1 + 1) * width, m2 * width:(m2 + 1) * width]
    return jnp.concatenate([prod[lags_ref[m]] for m in range(nlag)], axis=1).astype(jnp.bfloat16)


def pair_kernel(nlag, group, pairs_ref, lags_ref, lefts_ref, rights_ref, out_ref, lhs, rhs, prod):
    width = lefts_ref.shape[1]
    step = pl.program_id(0)

    @pl.when(step == 0)
    def _():
        @pl.loop(0, lefts_ref.shape[0])
        def _(r):
            for m, x in enumerate(left_stack(lefts_ref[r])):
                lhs[r, m * width:(m + 1) * width, :] = x

        @pl.loop(0, rights_ref.shape[0])
        def _(r):
            for m, x in enumerate(right_stack(rights_ref[r], nlag)):
                rhs[r, m * width:(m + 1) * width, :] = x

    for q in range(group):
        p = step * group + q
        out_ref[q] = one_pair(
            nlag, lags_ref, lhs[pairs_ref[p, 0]], rhs[pairs_ref[p, 1]], prod.at[q]
        )


def stream_kernel(nlag, pairs_ref, lags_ref, left_ref, right_ref, out_ref, prod):
    lhs = jnp.concatenate(left_stack(left_ref[0]), axis=0)
    rhs = jnp.concatenate(right_stack(right_ref[0], nlag), axis=0)
    out_ref[0] = one_pair(nlag, lags_ref, lhs, rhs, prod)


def covariances(lefts, rights, pairs, lags):
    npairs = pairs.shape[0]
    nlag = lags.shape[0]
    _, width, bins = lefts.shape
    out_shape = jax.ShapeDtypeStruct((npairs, width, nlag * width), jnp.bfloat16)
    panels = 3 * lefts.shape[0] + 5 * rights.shape[0]
    params = pltpu.CompilerParams(
        dimension_semantics=("arbitrary",), vmem_limit_bytes=48 << 20
    )
    if panels * width * bins * 2 <= 36 << 20:
        group = 4
        return pl.pallas_call(
            functools.partial(pair_kernel, nlag, group),
            grid_spec=pltpu.PrefetchScalarGridSpec(
                num_scalar_prefetch=2,
                grid=(npairs // group,),
                in_specs=[pl.BlockSpec(memory_space=pltpu.VMEM)] * 2,
                out_specs=pl.BlockSpec(
                    (group, width, nlag * width), lambda p, pairs, lags: (p, 0, 0)
                ),
                scratch_shapes=[
                    pltpu.VMEM((lefts.shape[0], 2 * width, bins), jnp.bfloat16),
                    pltpu.VMEM((rights.shape[0], nlag // 2 * width, bins), jnp.bfloat16),
                    pltpu.VMEM((group, nlag, width, width), jnp.float32),
                ],
            ),
            out_shape=out_shape,
            compiler_params=params,
        )(pairs, lags, lefts, rights)
    return pl.pallas_call(
        functools.partial(stream_kernel, nlag),
        grid_spec=pltpu.PrefetchScalarGridSpec(
            num_scalar_prefetch=2,
            grid=(npairs,),
            in_specs=[
                pl.BlockSpec((1, width, bins), lambda p, pairs, lags: (pairs[p, 0], 0, 0)),
                pl.BlockSpec((1, width, bins), lambda p, pairs, lags: (pairs[p, 1], 0, 0)),
            ],
            out_specs=pl.BlockSpec((1, width, nlag * width), lambda p, pairs, lags: (p, 0, 0)),
            scratch_shapes=[pltpu.VMEM((nlag, width, width), jnp.float32)],
        ),
        out_shape=out_shape,
        compiler_params=params,
    )(pairs, lags, lefts, rights)


def panels_kernel(
    shape, chunks, region_ref, basis_ref, act_ref, lefts_ref, rights_ref,
    own, send, landed, stage,
    rs_send, rs_recv, reg_send, reg_recv, col_send, col_recv,
    x_send, x_recv, sib_send, sib_recv, fwd_send, fwd_recv, left_sem, right_sem,
):
    nrow, ncol, nreg = shape
    nx = nrow // 2
    width = basis_ref.shape[1]
    bins = act_ref.shape[1]
    span = bins // chunks
    i, j, g = lax.axis_index("row"), lax.axis_index("col"), lax.axis_index("reg")
    x, core = i // 2, i % 2
    sib = x * 2 + 1 - core

    def reg_at(k):
        return {"reg": (g + k) % nreg}

    def col_at(k):
        return {"col": (j + k) % ncol}

    def x_at(k):
        return {"row": ((x + k) % nx) * 2 + core}

    peers = [reg_at(k) for k in range(1, nreg)]
    peers += [col_at(k) for k in range(1, ncol)]
    peers += [x_at(k) for k in range(1, nx)]
    peers += [{"row": sib}]
    barrier = pltpu.get_barrier_semaphore()
    for peer in peers:
        pl.semaphore_signal(
            barrier, inc=1, device_id=peer, device_id_type=pl.DeviceIdType.MESH
        )

    def remote(src, dst, send_sem, recv_sem, peer):
        return pltpu.make_async_remote_copy(
            src_ref=src, dst_ref=dst, send_sem=send_sem, recv_sem=recv_sem,
            device_id=peer, device_id_type=pl.DeviceIdType.MESH,
        )

    sent = []

    def start(*args):
        copy = remote(*args)
        copy.start()
        sent.append(copy)

    def right(row, region, c):
        return rights_ref.at[row * nreg + region, :, pl.ds(c * span, span)]

    def left(col, region, c):
        return lefts_ref.at[col * nreg + region, :, pl.ds(c * span, span)]

    pieces = []
    for n in range(basis_ref.shape[0] // BLK):
        block = basis_ref[n * BLK:(n + 1) * BLK, :]
        pieces.append(jnp.concatenate(
            [jnp.where(region_ref[n] == r, block, jnp.zeros_like(block)) for r in range(nreg)],
            axis=1,
        ))
    masked = jnp.concatenate(pieces, axis=0)

    def send_partials(c):
        part = lax.dot_general(
            masked, act_ref[:, c * span:(c + 1) * span], (((0,), (0,)), ((), ())),
            preferred_element_type=jnp.float32,
        )
        own[c] = part
        send[c] = part.astype(jnp.bfloat16)
        if c == 0:
            pl.semaphore_wait(barrier, len(peers))
        for k in range(1, nreg):
            rows = pl.ds(pl.multiple_of((g + k) % nreg * width, width), width)
            start(
                send.at[c, rows, :], landed.at[k - 1, c],
                rs_send.at[k - 1, c], rs_recv.at[k - 1, c], reg_at(k),
            )

    def spread(src, s, c):
        for k in range(1, nx):
            remote(src, right(i, s, c), x_send.at[k - 1, s, c], x_recv.at[k - 1, s, c], x_at(k)).start()
        for k in range(1, ncol):
            remote(src, left(j, s, c), col_send.at[k - 1, s, c], col_recv.at[k - 1, s, c], col_at(k)).start()
        remote(src, right(i, s, c), sib_send.at[s, c], sib_recv.at[s, c], {"row": sib}).start()
        pltpu.make_async_copy(src, left(j, s, c), left_sem.at[s, c]).start()

    def hop(src, s, d, c, way):
        to = g + 1 if way == 0 else g - 1
        return remote(
            src, right(i, s, c), reg_send.at[way, d, c], reg_recv.at[way, d, c], {"reg": to}
        )

    def onward(way, d):
        behind = g - d >= 0 if way == 0 else g + d < nreg
        ahead = g + 1 < nreg if way == 0 else g >= 1
        return jnp.logical_and(behind, ahead)

    def origin(way, d):
        return g - d if way == 0 else g + d

    def has(way, d):
        return g - d >= 0 if way == 0 else g + d < nreg

    def finish(c):
        total = own[c, pl.ds(pl.multiple_of(g * width, width), width), :]
        for k in range(1, nreg):
            remote(
                landed.at[k - 1, c], landed.at[k - 1, c],
                rs_send.at[k - 1, c], rs_recv.at[k - 1, c], reg_at(k),
            ).wait_recv()
            total = total + landed[k - 1, c].astype(jnp.float32)
        stage[c] = total.astype(jnp.bfloat16)
        for way in range(2):
            @pl.when(onward(way, 0))
            def _():
                hop(stage.at[c], g, 0, c, way).start()
        spread(stage.at[c], g, c)
        pltpu.make_async_copy(stage.at[c], right(i, g, c), right_sem.at[c]).start()

    def arrive(d, c):
        for way in range(2):
            @pl.when(has(way, d))
            def _():
                s = origin(way, d)
                here = right(i, s, c)
                hop(here, s, d - 1, c, way).wait_recv()
                if d < nreg - 1:
                    @pl.when(onward(way, d))
                    def _():
                        hop(here, s, d, c, way).start()
                spread(here, s, c)

    def pass_on(s, c):
        for k in range(1, nx):
            here = right((x - k + nx) % nx * 2 + core, s, c)
            remote(here, here, x_send.at[k - 1, s, c], x_recv.at[k - 1, s, c], x_at(k)).wait_recv()
            remote(here, here, fwd_send.at[k - 1, s, c], fwd_recv.at[k - 1, s, c], {"row": sib}).start()

    def cross(d, c):
        if d == 0:
            pass_on(g, c)
            return
        for way in range(2):
            @pl.when(has(way, d))
            def _():
                pass_on(origin(way, d), c)

    ahead = min(2, chunks)
    for c in range(ahead):
        send_partials(c)
    for tick in range(chunks + nreg):
        if tick < chunks:
            finish(tick)
            if tick + ahead < chunks:
                send_partials(tick + ahead)
        for d in range(1, nreg):
            if 0 <= tick - d < chunks:
                arrive(d, tick - d)
        for d in range(nreg):
            if 0 <= tick - d - 1 < chunks:
                cross(d, tick - d - 1)

    for c in range(chunks):
        pltpu.make_async_copy(stage.at[c], right(i, g, c), right_sem.at[c]).wait()
        for s in range(nreg):
            here = right(i, s, c)
            for k in range(1, ncol):
                there = left((j - k + ncol) % ncol, s, c)
                copy = remote(there, there, col_send.at[k - 1, s, c], col_recv.at[k - 1, s, c], col_at(k))
                copy.wait_recv()
                copy.wait_send()
            there = right(sib, s, c)
            copy = remote(there, there, sib_send.at[s, c], sib_recv.at[s, c], {"row": sib})
            copy.wait_recv()
            copy.wait_send()
            for k in range(1, nx):
                there = right((x - k + nx) % nx * 2 + 1 - core, s, c)
                copy = remote(there, there, fwd_send.at[k - 1, s, c], fwd_recv.at[k - 1, s, c], {"row": sib})
                copy.wait_recv()
                copy.wait_send()
                remote(here, here, x_send.at[k - 1, s, c], x_recv.at[k - 1, s, c], x_at(k)).wait_send()
            pltpu.make_async_copy(here, left(j, s, c), left_sem.at[s, c]).wait()
        for way in range(2):
            for d in range(nreg - 1):
                @pl.when(onward(way, d))
                def _():
                    s = origin(way, d)
                    hop(right(i, s, c), s, d, c, way).wait_send()
    for copy in sent:
        copy.wait_send()


def gathered_panels(shape, activity, basis, region_of):
    nrow, ncol, nreg = shape
    nx = nrow // 2
    width, bins = basis.shape[1], activity.shape[1]
    chunks = CHUNKS
    span = bins // chunks
    dma = pltpu.SemaphoreType.DMA
    return pl.pallas_call(
        functools.partial(panels_kernel, shape, chunks),
        in_specs=[
            pl.BlockSpec(memory_space=pltpu.SMEM),
            pl.BlockSpec(memory_space=pltpu.VMEM),
            pl.BlockSpec(memory_space=pltpu.VMEM),
        ],
        out_specs=[pl.BlockSpec(memory_space=pl.ANY)] * 2,
        out_shape=[
            jax.ShapeDtypeStruct((ncol * nreg, width, bins), jnp.bfloat16),
            jax.ShapeDtypeStruct((nrow * nreg, width, bins), jnp.bfloat16),
        ],
        scratch_shapes=[
            pltpu.VMEM((chunks, nreg * width, span), jnp.float32),
            pltpu.VMEM((chunks, nreg * width, span), jnp.bfloat16),
            pltpu.VMEM((nreg - 1, chunks, width, span), jnp.bfloat16),
            pltpu.VMEM((chunks, width, span), jnp.bfloat16),
        ]
        + [dma((nreg - 1, chunks))] * 2
        + [dma((2, nreg - 1, chunks))] * 2
        + [dma((ncol - 1, nreg, chunks))] * 2
        + [dma((nx - 1, nreg, chunks))] * 2
        + [dma((nreg, chunks))] * 2
        + [dma((nx - 1, nreg, chunks))] * 2
        + [dma((nreg, chunks)), dma((chunks,))],
        compiler_params=pltpu.CompilerParams(
            collective_id=0, has_side_effects=True, vmem_limit_bytes=40 << 20
        ),
    )(region_of, basis, activity)


def local(shape, activity, basis, region_of, pairs, lags):
    lefts, rights = gathered_panels(shape, activity, basis, region_of)
    return covariances(lefts, rights, pairs, lags)


def solution(mesh):
    shape = (mesh.shape["row"], mesh.shape["col"], mesh.shape["reg"])
    return jax.shard_map(
        functools.partial(local, shape),
        mesh=mesh,
        in_specs=(
            P(("row", "col", "reg"), None),
            P(("row", "col", "reg"), None),
            P(("row", "col", "reg")),
            P(("row", "col", "reg"), None),
            P(),
        ),
        out_specs=P(("row", "col", "reg"), None, None),
        check_vma=False,
    )
```

```python
import functools

import jax
import jax.numpy as jnp
from jax import lax
from jax.experimental import pallas as pl
from jax.experimental.pallas import tpu as pltpu
from jax.sharding import PartitionSpec as P

BLK = 128
CHUNKS = 4
SPLIT = 4


def shifted(x, s):
    bins = x.shape[1]
    moved = pltpu.roll(x, (bins - s) % bins, 1)
    edge = moved[:, bins - BLK:] if s > 0 else moved[:, :BLK]
    col = lax.broadcasted_iota(jnp.int32, edge.shape, 1)
    if s > 0:
        edge = jnp.where(col < BLK - s, edge, jnp.zeros_like(edge))
        return jnp.concatenate([moved[:, :bins - BLK], edge], axis=1)
    edge = jnp.where(col >= -s, edge, jnp.zeros_like(edge))
    return jnp.concatenate([edge, moved[:, BLK:]], axis=1)


def left_stack(left):
    return [left] + [shifted(left, -s) for s in range(1, SPLIT)]


def right_stack(right, nlag):
    return [right] + [shifted(right, s) for s in range(SPLIT, nlag, SPLIT)]


def one_pair(nlag, lags_ref, lhs, rhs, prod):
    width, bins = lhs.shape[0] // SPLIT, lhs.shape[1]
    acc = lax.dot_general(
        lhs, rhs, (((1,), (1,)), ((), ())), preferred_element_type=jnp.float32
    )
    acc = acc * (1.0 / bins**0.5)
    for lag in range(nlag):
        m1, m2 = lag % SPLIT, lag // SPLIT
        prod[lag] = acc[m1 * width:(m1 + 1) * width, m2 * width:(m2 + 1) * width]
    return jnp.concatenate([prod[lags_ref[m]] for m in range(nlag)], axis=1).astype(jnp.bfloat16)


def pair_kernel(nlag, group, pairs_ref, lags_ref, lefts_ref, rights_ref, out_ref, lhs, rhs, prod):
    width = lefts_ref.shape[1]
    step = pl.program_id(0)

    @pl.when(step == 0)
    def _():
        @pl.loop(0, lefts_ref.shape[0])
        def _(r):
            for m, x in enumerate(left_stack(lefts_ref[r])):
                lhs[r, m * width:(m + 1) * width, :] = x

        @pl.loop(0, rights_ref.shape[0])
        def _(r):
            for m, x in enumerate(right_stack(rights_ref[r], nlag)):
                rhs[r, m * width:(m + 1) * width, :] = x

    for q in range(group):
        p = step * group + q
        out_ref[q] = one_pair(
            nlag, lags_ref, lhs[pairs_ref[p, 0]], rhs[pairs_ref[p, 1]], prod.at[q]
        )


def stream_kernel(nlag, pairs_ref, lags_ref, left_ref, right_ref, out_ref, prod):
    lhs = jnp.concatenate(left_stack(left_ref[0]), axis=0)
    rhs = jnp.concatenate(right_stack(right_ref[0], nlag), axis=0)
    out_ref[0] = one_pair(nlag, lags_ref, lhs, rhs, prod)


def covariances(lefts, rights, pairs, lags):
    npairs = pairs.shape[0]
    nlag = lags.shape[0]
    _, width, bins = lefts.shape
    out_shape = jax.ShapeDtypeStruct((npairs, width, nlag * width), jnp.bfloat16)
    panels = (1 + SPLIT) * lefts.shape[0] + (1 + nlag // SPLIT) * rights.shape[0]
    params = pltpu.CompilerParams(
        dimension_semantics=("arbitrary",), vmem_limit_bytes=48 << 20
    )
    if panels * width * bins * 2 <= 36 << 20:
        group = 8
        return pl.pallas_call(
            functools.partial(pair_kernel, nlag, group),
            grid_spec=pltpu.PrefetchScalarGridSpec(
                num_scalar_prefetch=2,
                grid=(npairs // group,),
                in_specs=[pl.BlockSpec(memory_space=pltpu.VMEM)] * 2,
                out_specs=pl.BlockSpec(
                    (group, width, nlag * width), lambda p, pairs, lags: (p, 0, 0)
                ),
                scratch_shapes=[
                    pltpu.VMEM((lefts.shape[0], SPLIT * width, bins), jnp.bfloat16),
                    pltpu.VMEM((rights.shape[0], nlag // SPLIT * width, bins), jnp.bfloat16),
                    pltpu.VMEM((group, nlag, width, width), jnp.float32),
                ],
            ),
            out_shape=out_shape,
            compiler_params=params,
        )(pairs, lags, lefts, rights)
    return pl.pallas_call(
        functools.partial(stream_kernel, nlag),
        grid_spec=pltpu.PrefetchScalarGridSpec(
            num_scalar_prefetch=2,
            grid=(npairs,),
            in_specs=[
                pl.BlockSpec((1, width, bins), lambda p, pairs, lags: (pairs[p, 0], 0, 0)),
                pl.BlockSpec((1, width, bins), lambda p, pairs, lags: (pairs[p, 1], 0, 0)),
            ],
            out_specs=pl.BlockSpec((1, width, nlag * width), lambda p, pairs, lags: (p, 0, 0)),
            scratch_shapes=[pltpu.VMEM((nlag, width, width), jnp.float32)],
        ),
        out_shape=out_shape,
        compiler_params=params,
    )(pairs, lags, lefts, rights)


def panels_kernel(
    shape, chunks, region_ref, basis_ref, act_ref, lefts_ref, rights_ref,
    own, send, landed, stage,
    rs_send, rs_recv, reg_send, reg_recv, col_send, col_recv,
    x_send, x_recv, sib_send, sib_recv, fwd_send, fwd_recv, left_sem, right_sem,
):
    nrow, ncol, nreg = shape
    nx = nrow // 2
    width = basis_ref.shape[1]
    bins = act_ref.shape[1]
    span = bins // chunks
    i, j, g = lax.axis_index("row"), lax.axis_index("col"), lax.axis_index("reg")
    x, core = i // 2, i % 2
    sib = x * 2 + 1 - core

    def reg_at(k):
        return {"reg": (g + k) % nreg}

    def col_at(k):
        return {"col": (j + k) % ncol}

    def x_at(k):
        return {"row": ((x + k) % nx) * 2 + core}

    peers = [reg_at(k) for k in range(1, nreg)]
    peers += [col_at(k) for k in range(1, ncol)]
    peers += [x_at(k) for k in range(1, nx)]
    peers += [{"row": sib}]
    barrier = pltpu.get_barrier_semaphore()
    for peer in peers:
        pl.semaphore_signal(
            barrier, inc=1, device_id=peer, device_id_type=pl.DeviceIdType.MESH
        )

    def remote(src, dst, send_sem, recv_sem, peer):
        return pltpu.make_async_remote_copy(
            src_ref=src, dst_ref=dst, send_sem=send_sem, recv_sem=recv_sem,
            device_id=peer, device_id_type=pl.DeviceIdType.MESH,
        )

    sent = []

    def start(*args):
        copy = remote(*args)
        copy.start()
        sent.append(copy)

    def right(row, region, c):
        return rights_ref.at[row * nreg + region, :, pl.ds(c * span, span)]

    def left(col, region, c):
        return lefts_ref.at[col * nreg + region, :, pl.ds(c * span, span)]

    pieces = []
    for n in range(basis_ref.shape[0] // BLK):
        block = basis_ref[n * BLK:(n + 1) * BLK, :]
        pieces.append(jnp.concatenate(
            [jnp.where(region_ref[n] == r, block, jnp.zeros_like(block)) for r in range(nreg)],
            axis=1,
        ))
    masked = jnp.concatenate(pieces, axis=0)

    def send_partials(c):
        part = lax.dot_general(
            masked, act_ref[:, c * span:(c + 1) * span], (((0,), (0,)), ((), ())),
            preferred_element_type=jnp.float32,
        )
        own[c] = part
        send[c] = part.astype(jnp.bfloat16)
        if c == 0:
            pl.semaphore_wait(barrier, len(peers))
        for k in range(1, nreg):
            rows = pl.ds(pl.multiple_of((g + k) % nreg * width, width), width)
            start(
                send.at[c, rows, :], landed.at[k - 1, c],
                rs_send.at[k - 1, c], rs_recv.at[k - 1, c], reg_at(k),
            )

    def spread(src, s, c):
        for k in range(1, nx):
            remote(src, right(i, s, c), x_send.at[k - 1, s, c], x_recv.at[k - 1, s, c], x_at(k)).start()
        for k in range(1, ncol):
            remote(src, left(j, s, c), col_send.at[k - 1, s, c], col_recv.at[k - 1, s, c], col_at(k)).start()
        remote(src, right(i, s, c), sib_send.at[s, c], sib_recv.at[s, c], {"row": sib}).start()
        pltpu.make_async_copy(src, left(j, s, c), left_sem.at[s, c]).start()

    def hop(src, s, d, c, way):
        to = g + 1 if way == 0 else g - 1
        return remote(
            src, right(i, s, c), reg_send.at[way, d, c], reg_recv.at[way, d, c], {"reg": to}
        )

    def onward(way, d):
        behind = g - d >= 0 if way == 0 else g + d < nreg
        ahead = g + 1 < nreg if way == 0 else g >= 1
        return jnp.logical_and(behind, ahead)

    def origin(way, d):
        return g - d if way == 0 else g + d

    def has(way, d):
        return g - d >= 0 if way == 0 else g + d < nreg

    def finish(c):
        total = own[c, pl.ds(pl.multiple_of(g * width, width), width), :]
        for k in range(1, nreg):
            remote(
                landed.at[k - 1, c], landed.at[k - 1, c],
                rs_send.at[k - 1, c], rs_recv.at[k - 1, c], reg_at(k),
            ).wait_recv()
            total = total + landed[k - 1, c].astype(jnp.float32)
        stage[c] = total.astype(jnp.bfloat16)
        for way in range(2):
            @pl.when(onward(way, 0))
            def _():
                hop(stage.at[c], g, 0, c, way).start()
        spread(stage.at[c], g, c)
        pltpu.make_async_copy(stage.at[c], right(i, g, c), right_sem.at[c]).start()

    def arrive(d, c):
        for way in range(2):
            @pl.when(has(way, d))
            def _():
                s = origin(way, d)
                here = right(i, s, c)
                hop(here, s, d - 1, c, way).wait_recv()
                if d < nreg - 1:
                    @pl.when(onward(way, d))
                    def _():
                        hop(here, s, d, c, way).start()
                spread(here, s, c)

    def pass_on(s, c):
        for k in range(1, nx):
            here = right((x - k + nx) % nx * 2 + core, s, c)
            remote(here, here, x_send.at[k - 1, s, c], x_recv.at[k - 1, s, c], x_at(k)).wait_recv()
            remote(here, here, fwd_send.at[k - 1, s, c], fwd_recv.at[k - 1, s, c], {"row": sib}).start()

    def cross(d, c):
        if d == 0:
            pass_on(g, c)
            return
        for way in range(2):
            @pl.when(has(way, d))
            def _():
                pass_on(origin(way, d), c)

    ahead = min(2, chunks)
    for c in range(ahead):
        send_partials(c)
    for tick in range(chunks + nreg):
        if tick < chunks:
            finish(tick)
            if tick + ahead < chunks:
                send_partials(tick + ahead)
        for d in range(1, nreg):
            if 0 <= tick - d < chunks:
                arrive(d, tick - d)
        for d in range(nreg):
            if 0 <= tick - d - 1 < chunks:
                cross(d, tick - d - 1)

    for c in range(chunks):
        pltpu.make_async_copy(stage.at[c], right(i, g, c), right_sem.at[c]).wait()
        for s in range(nreg):
            here = right(i, s, c)
            for k in range(1, ncol):
                there = left((j - k + ncol) % ncol, s, c)
                copy = remote(there, there, col_send.at[k - 1, s, c], col_recv.at[k - 1, s, c], col_at(k))
                copy.wait_recv()
                copy.wait_send()
            there = right(sib, s, c)
            copy = remote(there, there, sib_send.at[s, c], sib_recv.at[s, c], {"row": sib})
            copy.wait_recv()
            copy.wait_send()
            for k in range(1, nx):
                there = right((x - k + nx) % nx * 2 + 1 - core, s, c)
                copy = remote(there, there, fwd_send.at[k - 1, s, c], fwd_recv.at[k - 1, s, c], {"row": sib})
                copy.wait_recv()
                copy.wait_send()
                remote(here, here, x_send.at[k - 1, s, c], x_recv.at[k - 1, s, c], x_at(k)).wait_send()
            pltpu.make_async_copy(here, left(j, s, c), left_sem.at[s, c]).wait()
        for way in range(2):
            for d in range(nreg - 1):
                @pl.when(onward(way, d))
                def _():
                    s = origin(way, d)
                    hop(right(i, s, c), s, d, c, way).wait_send()
    for copy in sent:
        copy.wait_send()


def gathered_panels(shape, activity, basis, region_of):
    nrow, ncol, nreg = shape
    nx = nrow // 2
    width, bins = basis.shape[1], activity.shape[1]
    chunks = CHUNKS
    span = bins // chunks
    dma = pltpu.SemaphoreType.DMA
    return pl.pallas_call(
        functools.partial(panels_kernel, shape, chunks),
        in_specs=[
            pl.BlockSpec(memory_space=pltpu.SMEM),
            pl.BlockSpec(memory_space=pltpu.VMEM),
            pl.BlockSpec(memory_space=pltpu.VMEM),
        ],
        out_specs=[pl.BlockSpec(memory_space=pl.ANY)] * 2,
        out_shape=[
            jax.ShapeDtypeStruct((ncol * nreg, width, bins), jnp.bfloat16),
            jax.ShapeDtypeStruct((nrow * nreg, width, bins), jnp.bfloat16),
        ],
        scratch_shapes=[
            pltpu.VMEM((chunks, nreg * width, span), jnp.float32),
            pltpu.VMEM((chunks, nreg * width, span), jnp.bfloat16),
            pltpu.VMEM((nreg - 1, chunks, width, span), jnp.bfloat16),
            pltpu.VMEM((chunks, width, span), jnp.bfloat16),
        ]
        + [dma((nreg - 1, chunks))] * 2
        + [dma((2, nreg - 1, chunks))] * 2
        + [dma((ncol - 1, nreg, chunks))] * 2
        + [dma((nx - 1, nreg, chunks))] * 2
        + [dma((nreg, chunks))] * 2
        + [dma((nx - 1, nreg, chunks))] * 2
        + [dma((nreg, chunks)), dma((chunks,))],
        compiler_params=pltpu.CompilerParams(
            collective_id=0, has_side_effects=True, vmem_limit_bytes=40 << 20
        ),
    )(region_of, basis, activity)


def local(shape, activity, basis, region_of, pairs, lags):
    lefts, rights = gathered_panels(shape, activity, basis, region_of)
    return covariances(lefts, rights, pairs, lags)


def solution(mesh):
    shape = (mesh.shape["row"], mesh.shape["col"], mesh.shape["reg"])
    return jax.shard_map(
        functools.partial(local, shape),
        mesh=mesh,
        in_specs=(
            P(("row", "col", "reg"), None),
            P(("row", "col", "reg"), None),
            P(("row", "col", "reg")),
            P(("row", "col", "reg"), None),
            P(),
        ),
        out_specs=P(("row", "col", "reg"), None, None),
        check_vma=False,
    )
```

```python
import functools

import jax
import jax.numpy as jnp
from jax import lax
from jax.experimental import pallas as pl
from jax.experimental.pallas import tpu as pltpu
from jax.sharding import PartitionSpec as P

BLK = 128
CHUNKS = 4
SPLIT = 4


def shifted(x, s):
    bins = x.shape[1]
    moved = pltpu.roll(x, (bins - s) % bins, 1)
    edge = moved[:, bins - BLK:] if s > 0 else moved[:, :BLK]
    col = lax.broadcasted_iota(jnp.int32, edge.shape, 1)
    if s > 0:
        edge = jnp.where(col < BLK - s, edge, jnp.zeros_like(edge))
        return jnp.concatenate([moved[:, :bins - BLK], edge], axis=1)
    edge = jnp.where(col >= -s, edge, jnp.zeros_like(edge))
    return jnp.concatenate([edge, moved[:, BLK:]], axis=1)


def left_stack(left):
    return [left] + [shifted(left, -s) for s in range(1, SPLIT)]


def right_stack(right, nlag):
    return [right] + [shifted(right, s) for s in range(SPLIT, nlag, SPLIT)]


def one_pair(nlag, lags_ref, lhs, rhs, prod):
    width, bins = lhs.shape[0] // SPLIT, lhs.shape[1]
    acc = lax.dot_general(
        lhs, rhs, (((1,), (1,)), ((), ())), preferred_element_type=jnp.float32
    )
    acc = acc * (1.0 / bins**0.5)
    for lag in range(nlag):
        m1, m2 = lag % SPLIT, lag // SPLIT
        prod[lag] = acc[m1 * width:(m1 + 1) * width, m2 * width:(m2 + 1) * width]
    return jnp.concatenate([prod[lags_ref[m]] for m in range(nlag)], axis=1).astype(jnp.bfloat16)


def pair_kernel(
    nlag, group, pairs_ref, lags_ref, lefts_ref, rights_ref, out_ref, lhs, rhs, prod,
    left_sem, right_sem,
):
    width = lefts_ref.shape[1]
    step = pl.program_id(0)

    @pl.when(step == 0)
    def _():
        def load_left(r):
            return pltpu.make_async_copy(lefts_ref.at[r], lhs.at[r, :width, :], left_sem.at[r])

        def load_right(r):
            return pltpu.make_async_copy(rights_ref.at[r], rhs.at[r, :width, :], right_sem.at[r])

        @pl.loop(0, lefts_ref.shape[0])
        def _(r):
            load_left(r).start()

        @pl.loop(0, rights_ref.shape[0])
        def _(r):
            load_right(r).start()

        @pl.loop(0, lefts_ref.shape[0])
        def _(r):
            load_left(r).wait()
            stack = left_stack(lhs[r, :width, :])
            for m in range(1, len(stack)):
                lhs[r, m * width:(m + 1) * width, :] = stack[m]

        @pl.loop(0, rights_ref.shape[0])
        def _(r):
            load_right(r).wait()
            stack = right_stack(rhs[r, :width, :], nlag)
            for m in range(1, len(stack)):
                rhs[r, m * width:(m + 1) * width, :] = stack[m]

    for q in range(group):
        p = step * group + q
        out_ref[q] = one_pair(
            nlag, lags_ref, lhs[pairs_ref[p, 0]], rhs[pairs_ref[p, 1]], prod.at[q]
        )


def stream_kernel(nlag, pairs_ref, lags_ref, left_ref, right_ref, out_ref, prod):
    lhs = jnp.concatenate(left_stack(left_ref[0]), axis=0)
    rhs = jnp.concatenate(right_stack(right_ref[0], nlag), axis=0)
    out_ref[0] = one_pair(nlag, lags_ref, lhs, rhs, prod)


def covariances(lefts, rights, pairs, lags):
    npairs = pairs.shape[0]
    nlag = lags.shape[0]
    _, width, bins = lefts.shape
    out_shape = jax.ShapeDtypeStruct((npairs, width, nlag * width), jnp.bfloat16)
    panels = (1 + SPLIT) * lefts.shape[0] + (1 + nlag // SPLIT) * rights.shape[0]
    params = pltpu.CompilerParams(
        dimension_semantics=("arbitrary",), vmem_limit_bytes=48 << 20
    )
    if panels * width * bins * 2 <= 36 << 20:
        group = 8
        return pl.pallas_call(
            functools.partial(pair_kernel, nlag, group),
            grid_spec=pltpu.PrefetchScalarGridSpec(
                num_scalar_prefetch=2,
                grid=(npairs // group,),
                in_specs=[pl.BlockSpec(memory_space=pltpu.HBM)] * 2,
                out_specs=pl.BlockSpec(
                    (group, width, nlag * width), lambda p, pairs, lags: (p, 0, 0)
                ),
                scratch_shapes=[
                    pltpu.VMEM((lefts.shape[0], SPLIT * width, bins), jnp.bfloat16),
                    pltpu.VMEM((rights.shape[0], nlag // SPLIT * width, bins), jnp.bfloat16),
                    pltpu.VMEM((group, nlag, width, width), jnp.float32),
                    pltpu.SemaphoreType.DMA((lefts.shape[0],)),
                    pltpu.SemaphoreType.DMA((rights.shape[0],)),
                ],
            ),
            out_shape=out_shape,
            compiler_params=params,
        )(pairs, lags, lefts, rights)
    return pl.pallas_call(
        functools.partial(stream_kernel, nlag),
        grid_spec=pltpu.PrefetchScalarGridSpec(
            num_scalar_prefetch=2,
            grid=(npairs,),
            in_specs=[
                pl.BlockSpec((1, width, bins), lambda p, pairs, lags: (pairs[p, 0], 0, 0)),
                pl.BlockSpec((1, width, bins), lambda p, pairs, lags: (pairs[p, 1], 0, 0)),
            ],
            out_specs=pl.BlockSpec((1, width, nlag * width), lambda p, pairs, lags: (p, 0, 0)),
            scratch_shapes=[pltpu.VMEM((nlag, width, width), jnp.float32)],
        ),
        out_shape=out_shape,
        compiler_params=params,
    )(pairs, lags, lefts, rights)


def panels_kernel(
    shape, chunks, region_ref, basis_ref, act_ref, lefts_ref, rights_ref,
    act, act_sem, own, send, landed, stage,
    rs_send, rs_recv, reg_send, reg_recv, col_send, col_recv,
    x_send, x_recv, sib_send, sib_recv, fwd_send, fwd_recv, left_sem, right_sem,
):
    nrow, ncol, nreg = shape
    nx = nrow // 2
    width = basis_ref.shape[1]
    bins = act_ref.shape[1]
    span = bins // chunks
    i, j, g = lax.axis_index("row"), lax.axis_index("col"), lax.axis_index("reg")
    x, core = i // 2, i % 2
    sib = x * 2 + 1 - core

    def reg_at(k):
        return {"reg": (g + k) % nreg}

    def col_at(k):
        return {"col": (j + k) % ncol}

    def x_at(k):
        return {"row": ((x + k) % nx) * 2 + core}

    peers = [reg_at(k) for k in range(1, nreg)]
    peers += [col_at(k) for k in range(1, ncol)]
    peers += [x_at(k) for k in range(1, nx)]
    peers += [{"row": sib}]
    loads = [
        pltpu.make_async_copy(
            act_ref.at[:, pl.ds(c * span, span)], act.at[c], act_sem.at[c]
        )
        for c in range(chunks)
    ]
    for load in loads:
        load.start()
    barrier = pltpu.get_barrier_semaphore()
    for peer in peers:
        pl.semaphore_signal(
            barrier, inc=1, device_id=peer, device_id_type=pl.DeviceIdType.MESH
        )

    def remote(src, dst, send_sem, recv_sem, peer):
        return pltpu.make_async_remote_copy(
            src_ref=src, dst_ref=dst, send_sem=send_sem, recv_sem=recv_sem,
            device_id=peer, device_id_type=pl.DeviceIdType.MESH,
        )

    sent = []

    def start(*args):
        copy = remote(*args)
        copy.start()
        sent.append(copy)

    def right(row, region, c):
        return rights_ref.at[row * nreg + region, :, pl.ds(c * span, span)]

    def left(col, region, c):
        return lefts_ref.at[col * nreg + region, :, pl.ds(c * span, span)]

    pieces = []
    for n in range(basis_ref.shape[0] // BLK):
        block = basis_ref[n * BLK:(n + 1) * BLK, :]
        pieces.append(jnp.concatenate(
            [jnp.where(region_ref[n] == r, block, jnp.zeros_like(block)) for r in range(nreg)],
            axis=1,
        ))
    masked = jnp.concatenate(pieces, axis=0)

    def send_partials(c):
        loads[c].wait()
        part = lax.dot_general(
            masked, act[c], (((0,), (0,)), ((), ())),
            preferred_element_type=jnp.float32,
        )
        own[c] = part
        send[c] = part.astype(jnp.bfloat16)
        if c == 0:
            pl.semaphore_wait(barrier, len(peers))
        for k in range(1, nreg):
            rows = pl.ds(pl.multiple_of((g + k) % nreg * width, width), width)
            start(
                send.at[c, rows, :], landed.at[k - 1, c],
                rs_send.at[k - 1, c], rs_recv.at[k - 1, c], reg_at(k),
            )

    def spread(src, s, c):
        for k in range(1, nx):
            remote(src, right(i, s, c), x_send.at[k - 1, s, c], x_recv.at[k - 1, s, c], x_at(k)).start()
        for k in range(1, ncol):
            remote(src, left(j, s, c), col_send.at[k - 1, s, c], col_recv.at[k - 1, s, c], col_at(k)).start()
        remote(src, right(i, s, c), sib_send.at[s, c], sib_recv.at[s, c], {"row": sib}).start()
        pltpu.make_async_copy(src, left(j, s, c), left_sem.at[s, c]).start()

    def hop(src, s, d, c, way):
        to = g + 1 if way == 0 else g - 1
        return remote(
            src, right(i, s, c), reg_send.at[way, d, c], reg_recv.at[way, d, c], {"reg": to}
        )

    def onward(way, d):
        behind = g - d >= 0 if way == 0 else g + d < nreg
        ahead = g + 1 < nreg if way == 0 else g >= 1
        return jnp.logical_and(behind, ahead)

    def origin(way, d):
        return g - d if way == 0 else g + d

    def has(way, d):
        return g - d >= 0 if way == 0 else g + d < nreg

    def finish(c):
        total = own[c, pl.ds(pl.multiple_of(g * width, width), width), :]
        for k in range(1, nreg):
            remote(
                landed.at[k - 1, c], landed.at[k - 1, c],
                rs_send.at[k - 1, c], rs_recv.at[k - 1, c], reg_at(k),
            ).wait_recv()
            total = total + landed[k - 1, c].astype(jnp.float32)
        stage[c] = total.astype(jnp.bfloat16)
        for way in range(2):
            @pl.when(onward(way, 0))
            def _():
                hop(stage.at[c], g, 0, c, way).start()
        spread(stage.at[c], g, c)
        pltpu.make_async_copy(stage.at[c], right(i, g, c), right_sem.at[c]).start()

    def arrive(d, c):
        for way in range(2):
            @pl.when(has(way, d))
            def _():
                s = origin(way, d)
                here = right(i, s, c)
                hop(here, s, d - 1, c, way).wait_recv()
                if d < nreg - 1:
                    @pl.when(onward(way, d))
                    def _():
                        hop(here, s, d, c, way).start()
                spread(here, s, c)

    def pass_on(s, c):
        for k in range(1, nx):
            here = right((x - k + nx) % nx * 2 + core, s, c)
            remote(here, here, x_send.at[k - 1, s, c], x_recv.at[k - 1, s, c], x_at(k)).wait_recv()
            remote(here, here, fwd_send.at[k - 1, s, c], fwd_recv.at[k - 1, s, c], {"row": sib}).start()

    def cross(d, c):
        if d == 0:
            pass_on(g, c)
            return
        for way in range(2):
            @pl.when(has(way, d))
            def _():
                pass_on(origin(way, d), c)

    ahead = min(2, chunks)
    for c in range(ahead):
        send_partials(c)
    for tick in range(chunks + nreg):
        if tick < chunks:
            finish(tick)
            if tick + ahead < chunks:
                send_partials(tick + ahead)
        for d in range(1, nreg):
            if 0 <= tick - d < chunks:
                arrive(d, tick - d)
        for d in range(nreg):
            if 0 <= tick - d - 1 < chunks:
                cross(d, tick - d - 1)

    for c in range(chunks):
        pltpu.make_async_copy(stage.at[c], right(i, g, c), right_sem.at[c]).wait()
        for s in range(nreg):
            here = right(i, s, c)
            for k in range(1, ncol):
                there = left((j - k + ncol) % ncol, s, c)
                copy = remote(there, there, col_send.at[k - 1, s, c], col_recv.at[k - 1, s, c], col_at(k))
                copy.wait_recv()
                copy.wait_send()
            there = right(sib, s, c)
            copy = remote(there, there, sib_send.at[s, c], sib_recv.at[s, c], {"row": sib})
            copy.wait_recv()
            copy.wait_send()
            for k in range(1, nx):
                there = right((x - k + nx) % nx * 2 + 1 - core, s, c)
                copy = remote(there, there, fwd_send.at[k - 1, s, c], fwd_recv.at[k - 1, s, c], {"row": sib})
                copy.wait_recv()
                copy.wait_send()
                remote(here, here, x_send.at[k - 1, s, c], x_recv.at[k - 1, s, c], x_at(k)).wait_send()
            pltpu.make_async_copy(here, left(j, s, c), left_sem.at[s, c]).wait()
        for way in range(2):
            for d in range(nreg - 1):
                @pl.when(onward(way, d))
                def _():
                    s = origin(way, d)
                    hop(right(i, s, c), s, d, c, way).wait_send()
    for copy in sent:
        copy.wait_send()


def gathered_panels(shape, activity, basis, region_of):
    nrow, ncol, nreg = shape
    nx = nrow // 2
    width, bins = basis.shape[1], activity.shape[1]
    chunks = CHUNKS
    span = bins // chunks
    dma = pltpu.SemaphoreType.DMA
    return pl.pallas_call(
        functools.partial(panels_kernel, shape, chunks),
        in_specs=[
            pl.BlockSpec(memory_space=pltpu.SMEM),
            pl.BlockSpec(memory_space=pltpu.VMEM),
            pl.BlockSpec(memory_space=pltpu.HBM),
        ],
        out_specs=[pl.BlockSpec(memory_space=pl.ANY)] * 2,
        out_shape=[
            jax.ShapeDtypeStruct((ncol * nreg, width, bins), jnp.bfloat16),
            jax.ShapeDtypeStruct((nrow * nreg, width, bins), jnp.bfloat16),
        ],
        scratch_shapes=[
            pltpu.VMEM((chunks, activity.shape[0], span), jnp.bfloat16),
            dma((chunks,)),
            pltpu.VMEM((chunks, nreg * width, span), jnp.float32),
            pltpu.VMEM((chunks, nreg * width, span), jnp.bfloat16),
            pltpu.VMEM((nreg - 1, chunks, width, span), jnp.bfloat16),
            pltpu.VMEM((chunks, width, span), jnp.bfloat16),
        ]
        + [dma((nreg - 1, chunks))] * 2
        + [dma((2, nreg - 1, chunks))] * 2
        + [dma((ncol - 1, nreg, chunks))] * 2
        + [dma((nx - 1, nreg, chunks))] * 2
        + [dma((nreg, chunks))] * 2
        + [dma((nx - 1, nreg, chunks))] * 2
        + [dma((nreg, chunks)), dma((chunks,))],
        compiler_params=pltpu.CompilerParams(
            collective_id=0, has_side_effects=True, vmem_limit_bytes=40 << 20
        ),
    )(region_of, basis, activity)


def local(shape, activity, basis, region_of, pairs, lags):
    lefts, rights = gathered_panels(shape, activity, basis, region_of)
    return covariances(lefts, rights, pairs, lags)


def solution(mesh):
    shape = (mesh.shape["row"], mesh.shape["col"], mesh.shape["reg"])
    return jax.shard_map(
        functools.partial(local, shape),
        mesh=mesh,
        in_specs=(
            P(("row", "col", "reg"), None),
            P(("row", "col", "reg"), None),
            P(("row", "col", "reg")),
            P(("row", "col", "reg"), None),
            P(),
        ),
        out_specs=P(("row", "col", "reg"), None, None),
        check_vma=False,
    )
```

```python
import functools

import jax
import jax.numpy as jnp
from jax import lax
from jax.experimental import pallas as pl
from jax.experimental.pallas import tpu as pltpu
from jax.sharding import PartitionSpec as P

BLK = 128
CHUNKS = 4
SPLIT = 4


def shifted(x, s):
    bins = x.shape[1]
    moved = pltpu.roll(x, (bins - s) % bins, 1)
    edge = moved[:, bins - BLK:] if s > 0 else moved[:, :BLK]
    col = lax.broadcasted_iota(jnp.int32, edge.shape, 1)
    if s > 0:
        edge = jnp.where(col < BLK - s, edge, jnp.zeros_like(edge))
        return jnp.concatenate([moved[:, :bins - BLK], edge], axis=1)
    edge = jnp.where(col >= -s, edge, jnp.zeros_like(edge))
    return jnp.concatenate([edge, moved[:, BLK:]], axis=1)


def left_stack(left):
    return [left] + [shifted(left, -s) for s in range(1, SPLIT)]


def right_stack(right, nlag):
    return [right] + [shifted(right, s) for s in range(SPLIT, nlag, SPLIT)]


def one_pair(nlag, lags_ref, lhs, rhs, prod):
    width, bins = lhs.shape[0] // SPLIT, lhs.shape[1]
    acc = lax.dot_general(
        lhs, rhs, (((1,), (1,)), ((), ())), preferred_element_type=jnp.float32
    )
    acc = acc * (1.0 / bins**0.5)
    for lag in range(nlag):
        m1, m2 = lag % SPLIT, lag // SPLIT
        prod[lag] = acc[m1 * width:(m1 + 1) * width, m2 * width:(m2 + 1) * width]
    return jnp.concatenate([prod[lags_ref[m]] for m in range(nlag)], axis=1).astype(jnp.bfloat16)


def pair_kernel(
    nlag, group, pairs_ref, lags_ref, lefts_ref, rights_ref, out_ref, lhs, rhs, prod,
    left_sem, right_sem,
):
    width = lefts_ref.shape[1]
    step = pl.program_id(0)

    @pl.when(step == 0)
    def _():
        def load_left(r):
            return pltpu.make_async_copy(lefts_ref.at[r], lhs.at[r, :width, :], left_sem.at[r])

        def load_right(r):
            return pltpu.make_async_copy(rights_ref.at[r], rhs.at[r, :width, :], right_sem.at[r])

        @pl.loop(0, lefts_ref.shape[0])
        def _(r):
            load_left(r).start()

        @pl.loop(0, rights_ref.shape[0])
        def _(r):
            load_right(r).start()

        @pl.loop(0, lefts_ref.shape[0])
        def _(r):
            load_left(r).wait()
            stack = left_stack(lhs[r, :width, :])
            for m in range(1, len(stack)):
                lhs[r, m * width:(m + 1) * width, :] = stack[m]

        @pl.loop(0, rights_ref.shape[0])
        def _(r):
            load_right(r).wait()
            stack = right_stack(rhs[r, :width, :], nlag)
            for m in range(1, len(stack)):
                rhs[r, m * width:(m + 1) * width, :] = stack[m]

    for q in range(group):
        p = step * group + q
        out_ref[q] = one_pair(
            nlag, lags_ref, lhs[pairs_ref[p, 0]], rhs[pairs_ref[p, 1]], prod.at[q]
        )


def stream_kernel(nlag, pairs_ref, lags_ref, left_ref, right_ref, out_ref, prod):
    lhs = jnp.concatenate(left_stack(left_ref[0]), axis=0)
    rhs = jnp.concatenate(right_stack(right_ref[0], nlag), axis=0)
    out_ref[0] = one_pair(nlag, lags_ref, lhs, rhs, prod)


def covariances(lefts, rights, pairs, lags):
    npairs = pairs.shape[0]
    nlag = lags.shape[0]
    _, width, bins = lefts.shape
    out_shape = jax.ShapeDtypeStruct((npairs, width, nlag * width), jnp.bfloat16)
    panels = (1 + SPLIT) * lefts.shape[0] + (1 + nlag // SPLIT) * rights.shape[0]
    params = pltpu.CompilerParams(
        dimension_semantics=("arbitrary",), vmem_limit_bytes=62 << 20
    )
    if panels * width * bins * 2 <= 36 << 20:
        group = 8
        return pl.pallas_call(
            functools.partial(pair_kernel, nlag, group),
            grid_spec=pltpu.PrefetchScalarGridSpec(
                num_scalar_prefetch=2,
                grid=(npairs // group,),
                in_specs=[pl.BlockSpec(memory_space=pltpu.HBM)] * 2,
                out_specs=pl.BlockSpec(
                    (group, width, nlag * width), lambda p, pairs, lags: (p, 0, 0)
                ),
                scratch_shapes=[
                    pltpu.VMEM((lefts.shape[0], SPLIT * width, bins), jnp.bfloat16),
                    pltpu.VMEM((rights.shape[0], nlag // SPLIT * width, bins), jnp.bfloat16),
                    pltpu.VMEM((group, nlag, width, width), jnp.float32),
                    pltpu.SemaphoreType.DMA((lefts.shape[0],)),
                    pltpu.SemaphoreType.DMA((rights.shape[0],)),
                ],
            ),
            out_shape=out_shape,
            compiler_params=params,
        )(pairs, lags, lefts, rights)
    return pl.pallas_call(
        functools.partial(stream_kernel, nlag),
        grid_spec=pltpu.PrefetchScalarGridSpec(
            num_scalar_prefetch=2,
            grid=(npairs,),
            in_specs=[
                pl.BlockSpec((1, width, bins), lambda p, pairs, lags: (pairs[p, 0], 0, 0)),
                pl.BlockSpec((1, width, bins), lambda p, pairs, lags: (pairs[p, 1], 0, 0)),
            ],
            out_specs=pl.BlockSpec((1, width, nlag * width), lambda p, pairs, lags: (p, 0, 0)),
            scratch_shapes=[pltpu.VMEM((nlag, width, width), jnp.float32)],
        ),
        out_shape=out_shape,
        compiler_params=params,
    )(pairs, lags, lefts, rights)


def panels_kernel(
    shape, chunks, region_ref, basis_ref, act_ref, lefts_ref, rights_ref,
    act, act_sem, own, send, landed, stage,
    rs_send, rs_recv, reg_send, reg_recv, col_send, col_recv,
    x_send, x_recv, sib_send, sib_recv, fwd_send, fwd_recv, left_sem, right_sem,
):
    nrow, ncol, nreg = shape
    nx = nrow // 2
    width = basis_ref.shape[1]
    bins = act_ref.shape[1]
    span = bins // chunks
    i, j, g = lax.axis_index("row"), lax.axis_index("col"), lax.axis_index("reg")
    x, core = i // 2, i % 2
    sib = x * 2 + 1 - core

    def reg_at(k):
        return {"reg": (g + k) % nreg}

    def col_at(k):
        return {"col": (j + k) % ncol}

    def x_at(k):
        return {"row": ((x + k) % nx) * 2 + core}

    peers = [reg_at(k) for k in range(1, nreg)]
    peers += [col_at(k) for k in range(1, ncol)]
    peers += [x_at(k) for k in range(1, nx)]
    peers += [{"row": sib}]
    loads = [
        pltpu.make_async_copy(
            act_ref.at[:, pl.ds(c * span, span)], act.at[c], act_sem.at[c]
        )
        for c in range(chunks)
    ]
    for load in loads:
        load.start()
    barrier = pltpu.get_barrier_semaphore()
    for peer in peers:
        pl.semaphore_signal(
            barrier, inc=1, device_id=peer, device_id_type=pl.DeviceIdType.MESH
        )

    def remote(src, dst, send_sem, recv_sem, peer):
        return pltpu.make_async_remote_copy(
            src_ref=src, dst_ref=dst, send_sem=send_sem, recv_sem=recv_sem,
            device_id=peer, device_id_type=pl.DeviceIdType.MESH,
        )

    sent = []

    def start(*args):
        copy = remote(*args)
        copy.start()
        sent.append(copy)

    def right(row, region, c):
        return rights_ref.at[row * nreg + region, :, pl.ds(c * span, span)]

    def left(col, region, c):
        return lefts_ref.at[col * nreg + region, :, pl.ds(c * span, span)]

    pieces = []
    for n in range(basis_ref.shape[0] // BLK):
        block = basis_ref[n * BLK:(n + 1) * BLK, :]
        pieces.append(jnp.concatenate(
            [jnp.where(region_ref[n] == r, block, jnp.zeros_like(block)) for r in range(nreg)],
            axis=1,
        ))
    masked = jnp.concatenate(pieces, axis=0)

    def send_partials(c):
        loads[c].wait()
        part = lax.dot_general(
            masked, act[c], (((0,), (0,)), ((), ())),
            preferred_element_type=jnp.float32,
        )
        own[c] = part
        send[c] = part.astype(jnp.bfloat16)
        if c == 0:
            pl.semaphore_wait(barrier, len(peers))
        for k in range(1, nreg):
            rows = pl.ds(pl.multiple_of((g + k) % nreg * width, width), width)
            start(
                send.at[c, rows, :], landed.at[k - 1, c],
                rs_send.at[k - 1, c], rs_recv.at[k - 1, c], reg_at(k),
            )

    def spread(src, s, c):
        for k in range(1, nx):
            remote(src, right(i, s, c), x_send.at[k - 1, s, c], x_recv.at[k - 1, s, c], x_at(k)).start()
        for k in range(1, ncol):
            remote(src, left(j, s, c), col_send.at[k - 1, s, c], col_recv.at[k - 1, s, c], col_at(k)).start()
        remote(src, right(i, s, c), sib_send.at[s, c], sib_recv.at[s, c], {"row": sib}).start()
        pltpu.make_async_copy(src, left(j, s, c), left_sem.at[s, c]).start()

    def hop(src, s, d, c, way):
        to = g + 1 if way == 0 else g - 1
        return remote(
            src, right(i, s, c), reg_send.at[way, d, c], reg_recv.at[way, d, c], {"reg": to}
        )

    def onward(way, d):
        behind = g - d >= 0 if way == 0 else g + d < nreg
        ahead = g + 1 < nreg if way == 0 else g >= 1
        return jnp.logical_and(behind, ahead)

    def origin(way, d):
        return g - d if way == 0 else g + d

    def has(way, d):
        return g - d >= 0 if way == 0 else g + d < nreg

    def finish(c):
        total = own[c, pl.ds(pl.multiple_of(g * width, width), width), :]
        for k in range(1, nreg):
            remote(
                landed.at[k - 1, c], landed.at[k - 1, c],
                rs_send.at[k - 1, c], rs_recv.at[k - 1, c], reg_at(k),
            ).wait_recv()
            total = total + landed[k - 1, c].astype(jnp.float32)
        stage[c] = total.astype(jnp.bfloat16)
        for way in range(2):
            @pl.when(onward(way, 0))
            def _():
                hop(stage.at[c], g, 0, c, way).start()
        spread(stage.at[c], g, c)
        pltpu.make_async_copy(stage.at[c], right(i, g, c), right_sem.at[c]).start()

    def arrive(d, c):
        for way in range(2):
            @pl.when(has(way, d))
            def _():
                s = origin(way, d)
                here = right(i, s, c)
                hop(here, s, d - 1, c, way).wait_recv()
                if d < nreg - 1:
                    @pl.when(onward(way, d))
                    def _():
                        hop(here, s, d, c, way).start()
                spread(here, s, c)

    def pass_on(s, c):
        for k in range(1, nx):
            here = right((x - k + nx) % nx * 2 + core, s, c)
            remote(here, here, x_send.at[k - 1, s, c], x_recv.at[k - 1, s, c], x_at(k)).wait_recv()
            remote(here, here, fwd_send.at[k - 1, s, c], fwd_recv.at[k - 1, s, c], {"row": sib}).start()

    def cross(d, c):
        if d == 0:
            pass_on(g, c)
            return
        for way in range(2):
            @pl.when(has(way, d))
            def _():
                pass_on(origin(way, d), c)

    ahead = min(2, chunks)
    for c in range(ahead):
        send_partials(c)
    for tick in range(chunks + nreg):
        if tick < chunks:
            finish(tick)
            if tick + ahead < chunks:
                send_partials(tick + ahead)
        for d in range(1, nreg):
            if 0 <= tick - d < chunks:
                arrive(d, tick - d)
        for d in range(nreg):
            if 0 <= tick - d - 1 < chunks:
                cross(d, tick - d - 1)

    for c in range(chunks):
        pltpu.make_async_copy(stage.at[c], right(i, g, c), right_sem.at[c]).wait()
        for s in range(nreg):
            here = right(i, s, c)
            for k in range(1, ncol):
                there = left((j - k + ncol) % ncol, s, c)
                copy = remote(there, there, col_send.at[k - 1, s, c], col_recv.at[k - 1, s, c], col_at(k))
                copy.wait_recv()
                copy.wait_send()
            there = right(sib, s, c)
            copy = remote(there, there, sib_send.at[s, c], sib_recv.at[s, c], {"row": sib})
            copy.wait_recv()
            copy.wait_send()
            for k in range(1, nx):
                there = right((x - k + nx) % nx * 2 + 1 - core, s, c)
                copy = remote(there, there, fwd_send.at[k - 1, s, c], fwd_recv.at[k - 1, s, c], {"row": sib})
                copy.wait_recv()
                copy.wait_send()
                remote(here, here, x_send.at[k - 1, s, c], x_recv.at[k - 1, s, c], x_at(k)).wait_send()
            pltpu.make_async_copy(here, left(j, s, c), left_sem.at[s, c]).wait()
        for way in range(2):
            for d in range(nreg - 1):
                @pl.when(onward(way, d))
                def _():
                    s = origin(way, d)
                    hop(right(i, s, c), s, d, c, way).wait_send()
    for copy in sent:
        copy.wait_send()


def gathered_panels(shape, activity, basis, region_of):
    nrow, ncol, nreg = shape
    nx = nrow // 2
    width, bins = basis.shape[1], activity.shape[1]
    chunks = CHUNKS
    span = bins // chunks
    dma = pltpu.SemaphoreType.DMA
    return pl.pallas_call(
        functools.partial(panels_kernel, shape, chunks),
        in_specs=[
            pl.BlockSpec(memory_space=pltpu.SMEM),
            pl.BlockSpec(memory_space=pltpu.VMEM),
            pl.BlockSpec(memory_space=pltpu.HBM),
        ],
        out_specs=[pl.BlockSpec(memory_space=pl.ANY)] * 2,
        out_shape=[
            jax.ShapeDtypeStruct((ncol * nreg, width, bins), jnp.bfloat16),
            jax.ShapeDtypeStruct((nrow * nreg, width, bins), jnp.bfloat16),
        ],
        scratch_shapes=[
            pltpu.VMEM((chunks, activity.shape[0], span), jnp.bfloat16),
            dma((chunks,)),
            pltpu.VMEM((chunks, nreg * width, span), jnp.float32),
            pltpu.VMEM((chunks, nreg * width, span), jnp.bfloat16),
            pltpu.VMEM((nreg - 1, chunks, width, span), jnp.bfloat16),
            pltpu.VMEM((chunks, width, span), jnp.bfloat16),
        ]
        + [dma((nreg - 1, chunks))] * 2
        + [dma((2, nreg - 1, chunks))] * 2
        + [dma((ncol - 1, nreg, chunks))] * 2
        + [dma((nx - 1, nreg, chunks))] * 2
        + [dma((nreg, chunks))] * 2
        + [dma((nx - 1, nreg, chunks))] * 2
        + [dma((nreg, chunks)), dma((chunks,))],
        compiler_params=pltpu.CompilerParams(
            collective_id=0, has_side_effects=True, vmem_limit_bytes=62 << 20
        ),
    )(region_of, basis, activity)


def local(shape, activity, basis, region_of, pairs, lags):
    lefts, rights = gathered_panels(shape, activity, basis, region_of)
    return covariances(lefts, rights, pairs, lags)


def solution(mesh):
    shape = (mesh.shape["row"], mesh.shape["col"], mesh.shape["reg"])
    return jax.shard_map(
        functools.partial(local, shape),
        mesh=mesh,
        in_specs=(
            P(("row", "col", "reg"), None),
            P(("row", "col", "reg"), None),
            P(("row", "col", "reg")),
            P(("row", "col", "reg"), None),
            P(),
        ),
        out_specs=P(("row", "col", "reg"), None, None),
        check_vma=False,
    )
```

```python
import functools

import jax
import jax.numpy as jnp
from jax import lax
from jax.experimental import pallas as pl
from jax.experimental.pallas import tpu as pltpu
from jax.sharding import PartitionSpec as P

BLK = 128
CHUNKS = 8
SPLIT = 4


def shifted(x, s):
    bins = x.shape[1]
    moved = pltpu.roll(x, (bins - s) % bins, 1)
    edge = moved[:, bins - BLK:] if s > 0 else moved[:, :BLK]
    col = lax.broadcasted_iota(jnp.int32, edge.shape, 1)
    if s > 0:
        edge = jnp.where(col < BLK - s, edge, jnp.zeros_like(edge))
        return jnp.concatenate([moved[:, :bins - BLK], edge], axis=1)
    edge = jnp.where(col >= -s, edge, jnp.zeros_like(edge))
    return jnp.concatenate([edge, moved[:, BLK:]], axis=1)


def left_stack(left):
    return [left] + [shifted(left, -s) for s in range(1, SPLIT)]


def right_stack(right, nlag):
    return [right] + [shifted(right, s) for s in range(SPLIT, nlag, SPLIT)]


def one_pair(nlag, lags_ref, lhs, rhs, prod):
    width, bins = lhs.shape[0] // SPLIT, lhs.shape[1]
    acc = lax.dot_general(
        lhs, rhs, (((1,), (1,)), ((), ())), preferred_element_type=jnp.float32
    )
    acc = acc * (1.0 / bins**0.5)
    for lag in range(nlag):
        m1, m2 = lag % SPLIT, lag // SPLIT
        prod[lag] = acc[m1 * width:(m1 + 1) * width, m2 * width:(m2 + 1) * width]
    return jnp.concatenate([prod[lags_ref[m]] for m in range(nlag)], axis=1).astype(jnp.bfloat16)


def pair_kernel(
    nlag, group, pairs_ref, lags_ref, lefts_ref, rights_ref, out_ref, lhs, rhs, prod,
    left_sem, right_sem,
):
    width = lefts_ref.shape[1]
    step = pl.program_id(0)

    @pl.when(step == 0)
    def _():
        def load_left(r):
            return pltpu.make_async_copy(lefts_ref.at[r], lhs.at[r, :width, :], left_sem.at[r])

        def load_right(r):
            return pltpu.make_async_copy(rights_ref.at[r], rhs.at[r, :width, :], right_sem.at[r])

        @pl.loop(0, lefts_ref.shape[0])
        def _(r):
            load_left(r).start()

        @pl.loop(0, rights_ref.shape[0])
        def _(r):
            load_right(r).start()

        @pl.loop(0, lefts_ref.shape[0])
        def _(r):
            load_left(r).wait()
            stack = left_stack(lhs[r, :width, :])
            for m in range(1, len(stack)):
                lhs[r, m * width:(m + 1) * width, :] = stack[m]

        @pl.loop(0, rights_ref.shape[0])
        def _(r):
            load_right(r).wait()
            stack = right_stack(rhs[r, :width, :], nlag)
            for m in range(1, len(stack)):
                rhs[r, m * width:(m + 1) * width, :] = stack[m]

    for q in range(group):
        p = step * group + q
        out_ref[q] = one_pair(
            nlag, lags_ref, lhs[pairs_ref[p, 0]], rhs[pairs_ref[p, 1]], prod.at[q]
        )


def stream_kernel(nlag, pairs_ref, lags_ref, left_ref, right_ref, out_ref, prod):
    lhs = jnp.concatenate(left_stack(left_ref[0]), axis=0)
    rhs = jnp.concatenate(right_stack(right_ref[0], nlag), axis=0)
    out_ref[0] = one_pair(nlag, lags_ref, lhs, rhs, prod)


def covariances(lefts, rights, pairs, lags):
    npairs = pairs.shape[0]
    nlag = lags.shape[0]
    _, width, bins = lefts.shape
    out_shape = jax.ShapeDtypeStruct((npairs, width, nlag * width), jnp.bfloat16)
    panels = (1 + SPLIT) * lefts.shape[0] + (1 + nlag // SPLIT) * rights.shape[0]
    params = pltpu.CompilerParams(
        dimension_semantics=("arbitrary",), vmem_limit_bytes=62 << 20
    )
    if panels * width * bins * 2 <= 36 << 20:
        group = 8
        return pl.pallas_call(
            functools.partial(pair_kernel, nlag, group),
            grid_spec=pltpu.PrefetchScalarGridSpec(
                num_scalar_prefetch=2,
                grid=(npairs // group,),
                in_specs=[pl.BlockSpec(memory_space=pltpu.HBM)] * 2,
                out_specs=pl.BlockSpec(
                    (group, width, nlag * width), lambda p, pairs, lags: (p, 0, 0)
                ),
                scratch_shapes=[
                    pltpu.VMEM((lefts.shape[0], SPLIT * width, bins), jnp.bfloat16),
                    pltpu.VMEM((rights.shape[0], nlag // SPLIT * width, bins), jnp.bfloat16),
                    pltpu.VMEM((group, nlag, width, width), jnp.float32),
                    pltpu.SemaphoreType.DMA((lefts.shape[0],)),
                    pltpu.SemaphoreType.DMA((rights.shape[0],)),
                ],
            ),
            out_shape=out_shape,
            compiler_params=params,
        )(pairs, lags, lefts, rights)
    return pl.pallas_call(
        functools.partial(stream_kernel, nlag),
        grid_spec=pltpu.PrefetchScalarGridSpec(
            num_scalar_prefetch=2,
            grid=(npairs,),
            in_specs=[
                pl.BlockSpec((1, width, bins), lambda p, pairs, lags: (pairs[p, 0], 0, 0)),
                pl.BlockSpec((1, width, bins), lambda p, pairs, lags: (pairs[p, 1], 0, 0)),
            ],
            out_specs=pl.BlockSpec((1, width, nlag * width), lambda p, pairs, lags: (p, 0, 0)),
            scratch_shapes=[pltpu.VMEM((nlag, width, width), jnp.float32)],
        ),
        out_shape=out_shape,
        compiler_params=params,
    )(pairs, lags, lefts, rights)


def panels_kernel(
    shape, chunks, region_ref, basis_ref, act_ref, lefts_ref, rights_ref,
    act, act_sem, own, send, landed, stage,
    rs_send, rs_recv, reg_send, reg_recv, col_send, col_recv,
    x_send, x_recv, sib_send, sib_recv, fwd_send, fwd_recv, left_sem, right_sem,
):
    nrow, ncol, nreg = shape
    nx = nrow // 2
    width = basis_ref.shape[1]
    bins = act_ref.shape[1]
    span = bins // chunks
    i, j, g = lax.axis_index("row"), lax.axis_index("col"), lax.axis_index("reg")
    x, core = i // 2, i % 2
    sib = x * 2 + 1 - core

    def reg_at(k):
        return {"reg": (g + k) % nreg}

    def col_at(k):
        return {"col": (j + k) % ncol}

    def x_at(k):
        return {"row": ((x + k) % nx) * 2 + core}

    peers = [reg_at(k) for k in range(1, nreg)]
    peers += [col_at(k) for k in range(1, ncol)]
    peers += [x_at(k) for k in range(1, nx)]
    peers += [{"row": sib}]
    loads = [
        pltpu.make_async_copy(
            act_ref.at[:, pl.ds(c * span, span)], act.at[c], act_sem.at[c]
        )
        for c in range(chunks)
    ]
    for load in loads:
        load.start()
    barrier = pltpu.get_barrier_semaphore()
    for peer in peers:
        pl.semaphore_signal(
            barrier, inc=1, device_id=peer, device_id_type=pl.DeviceIdType.MESH
        )

    def remote(src, dst, send_sem, recv_sem, peer):
        return pltpu.make_async_remote_copy(
            src_ref=src, dst_ref=dst, send_sem=send_sem, recv_sem=recv_sem,
            device_id=peer, device_id_type=pl.DeviceIdType.MESH,
        )

    sent = []

    def start(*args):
        copy = remote(*args)
        copy.start()
        sent.append(copy)

    def right(row, region, c):
        return rights_ref.at[row * nreg + region, :, pl.ds(c * span, span)]

    def left(col, region, c):
        return lefts_ref.at[col * nreg + region, :, pl.ds(c * span, span)]

    pieces = []
    for n in range(basis_ref.shape[0] // BLK):
        block = basis_ref[n * BLK:(n + 1) * BLK, :]
        pieces.append(jnp.concatenate(
            [jnp.where(region_ref[n] == r, block, jnp.zeros_like(block)) for r in range(nreg)],
            axis=1,
        ))
    masked = jnp.concatenate(pieces, axis=0)

    def send_partials(c):
        loads[c].wait()
        part = lax.dot_general(
            masked, act[c], (((0,), (0,)), ((), ())),
            preferred_element_type=jnp.float32,
        )
        own[c] = part
        send[c] = part.astype(jnp.bfloat16)
        if c == 0:
            pl.semaphore_wait(barrier, len(peers))
        for k in range(1, nreg):
            rows = pl.ds(pl.multiple_of((g + k) % nreg * width, width), width)
            start(
                send.at[c, rows, :], landed.at[k - 1, c],
                rs_send.at[k - 1, c], rs_recv.at[k - 1, c], reg_at(k),
            )

    def spread(src, s, c):
        for k in range(1, nx):
            remote(src, right(i, s, c), x_send.at[k - 1, s, c], x_recv.at[k - 1, s, c], x_at(k)).start()
        for k in range(1, ncol):
            remote(src, left(j, s, c), col_send.at[k - 1, s, c], col_recv.at[k - 1, s, c], col_at(k)).start()
        remote(src, right(i, s, c), sib_send.at[s, c], sib_recv.at[s, c], {"row": sib}).start()
        pltpu.make_async_copy(src, left(j, s, c), left_sem.at[s, c]).start()

    def hop(src, s, d, c, way):
        to = g + 1 if way == 0 else g - 1
        return remote(
            src, right(i, s, c), reg_send.at[way, d, c], reg_recv.at[way, d, c], {"reg": to}
        )

    def onward(way, d):
        behind = g - d >= 0 if way == 0 else g + d < nreg
        ahead = g + 1 < nreg if way == 0 else g >= 1
        return jnp.logical_and(behind, ahead)

    def origin(way, d):
        return g - d if way == 0 else g + d

    def has(way, d):
        return g - d >= 0 if way == 0 else g + d < nreg

    def finish(c):
        total = own[c, pl.ds(pl.multiple_of(g * width, width), width), :]
        for k in range(1, nreg):
            remote(
                landed.at[k - 1, c], landed.at[k - 1, c],
                rs_send.at[k - 1, c], rs_recv.at[k - 1, c], reg_at(k),
            ).wait_recv()
            total = total + landed[k - 1, c].astype(jnp.float32)
        stage[c] = total.astype(jnp.bfloat16)
        for way in range(2):
            @pl.when(onward(way, 0))
            def _():
                hop(stage.at[c], g, 0, c, way).start()
        spread(stage.at[c], g, c)
        pltpu.make_async_copy(stage.at[c], right(i, g, c), right_sem.at[c]).start()

    def arrive(d, c):
        for way in range(2):
            @pl.when(has(way, d))
            def _():
                s = origin(way, d)
                here = right(i, s, c)
                hop(here, s, d - 1, c, way).wait_recv()
                if d < nreg - 1:
                    @pl.when(onward(way, d))
                    def _():
                        hop(here, s, d, c, way).start()
                spread(here, s, c)

    def pass_on(s, c):
        for k in range(1, nx):
            here = right((x - k + nx) % nx * 2 + core, s, c)
            remote(here, here, x_send.at[k - 1, s, c], x_recv.at[k - 1, s, c], x_at(k)).wait_recv()
            remote(here, here, fwd_send.at[k - 1, s, c], fwd_recv.at[k - 1, s, c], {"row": sib}).start()

    def cross(d, c):
        if d == 0:
            pass_on(g, c)
            return
        for way in range(2):
            @pl.when(has(way, d))
            def _():
                pass_on(origin(way, d), c)

    ahead = min(4, chunks)
    for c in range(ahead):
        send_partials(c)
    for tick in range(chunks + nreg):
        if tick < chunks:
            finish(tick)
            if tick + ahead < chunks:
                send_partials(tick + ahead)
        for d in range(1, nreg):
            if 0 <= tick - d < chunks:
                arrive(d, tick - d)
        for d in range(nreg):
            if 0 <= tick - d - 1 < chunks:
                cross(d, tick - d - 1)

    for c in range(chunks):
        pltpu.make_async_copy(stage.at[c], right(i, g, c), right_sem.at[c]).wait()
        for s in range(nreg):
            here = right(i, s, c)
            for k in range(1, ncol):
                there = left((j - k + ncol) % ncol, s, c)
                copy = remote(there, there, col_send.at[k - 1, s, c], col_recv.at[k - 1, s, c], col_at(k))
                copy.wait_recv()
                copy.wait_send()
            there = right(sib, s, c)
            copy = remote(there, there, sib_send.at[s, c], sib_recv.at[s, c], {"row": sib})
            copy.wait_recv()
            copy.wait_send()
            for k in range(1, nx):
                there = right((x - k + nx) % nx * 2 + 1 - core, s, c)
                copy = remote(there, there, fwd_send.at[k - 1, s, c], fwd_recv.at[k - 1, s, c], {"row": sib})
                copy.wait_recv()
                copy.wait_send()
                remote(here, here, x_send.at[k - 1, s, c], x_recv.at[k - 1, s, c], x_at(k)).wait_send()
            pltpu.make_async_copy(here, left(j, s, c), left_sem.at[s, c]).wait()
        for way in range(2):
            for d in range(nreg - 1):
                @pl.when(onward(way, d))
                def _():
                    s = origin(way, d)
                    hop(right(i, s, c), s, d, c, way).wait_send()
    for copy in sent:
        copy.wait_send()


def gathered_panels(shape, activity, basis, region_of):
    nrow, ncol, nreg = shape
    nx = nrow // 2
    width, bins = basis.shape[1], activity.shape[1]
    chunks = CHUNKS
    span = bins // chunks
    dma = pltpu.SemaphoreType.DMA
    return pl.pallas_call(
        functools.partial(panels_kernel, shape, chunks),
        in_specs=[
            pl.BlockSpec(memory_space=pltpu.SMEM),
            pl.BlockSpec(memory_space=pltpu.VMEM),
            pl.BlockSpec(memory_space=pltpu.HBM),
        ],
        out_specs=[pl.BlockSpec(memory_space=pl.ANY)] * 2,
        out_shape=[
            jax.ShapeDtypeStruct((ncol * nreg, width, bins), jnp.bfloat16),
            jax.ShapeDtypeStruct((nrow * nreg, width, bins), jnp.bfloat16),
        ],
        scratch_shapes=[
            pltpu.VMEM((chunks, activity.shape[0], span), jnp.bfloat16),
            dma((chunks,)),
            pltpu.VMEM((chunks, nreg * width, span), jnp.float32),
            pltpu.VMEM((chunks, nreg * width, span), jnp.bfloat16),
            pltpu.VMEM((nreg - 1, chunks, width, span), jnp.bfloat16),
            pltpu.VMEM((chunks, width, span), jnp.bfloat16),
        ]
        + [dma((nreg - 1, chunks))] * 2
        + [dma((2, nreg - 1, chunks))] * 2
        + [dma((ncol - 1, nreg, chunks))] * 2
        + [dma((nx - 1, nreg, chunks))] * 2
        + [dma((nreg, chunks))] * 2
        + [dma((nx - 1, nreg, chunks))] * 2
        + [dma((nreg, chunks)), dma((chunks,))],
        compiler_params=pltpu.CompilerParams(
            collective_id=0, has_side_effects=True, vmem_limit_bytes=62 << 20
        ),
    )(region_of, basis, activity)


def local(shape, activity, basis, region_of, pairs, lags):
    lefts, rights = gathered_panels(shape, activity, basis, region_of)
    return covariances(lefts, rights, pairs, lags)


def solution(mesh):
    shape = (mesh.shape["row"], mesh.shape["col"], mesh.shape["reg"])
    return jax.shard_map(
        functools.partial(local, shape),
        mesh=mesh,
        in_specs=(
            P(("row", "col", "reg"), None),
            P(("row", "col", "reg"), None),
            P(("row", "col", "reg")),
            P(("row", "col", "reg"), None),
            P(),
        ),
        out_specs=P(("row", "col", "reg"), None, None),
        check_vma=False,
    )
```
